128 devices in a mesh: dp: 8 (over x, y_lo), mp: 16 (over z, y_hi, core).
Axes of the slice: x: 4, y: 4 (y_hi: 2, y_lo: 2; y = y_hi * 2 + y_lo), z: 4, core: 2. Of those that a mesh axis runs over, the one named last changes fastest.
Arguments:
- features: bfloat16 [16384, 16384], P('dp', 'mp'), may hold values from -6 to 6
- weights: bfloat16 [16384, 16384], P('mp', 'dp'), may hold values from -6 to 6
- u_rows: float32 [1024, 16384], P('mp', 'dp'), as said below
- keep_pairs: int32 [2, 128, 2], replicated, may hold values from 0 to 3, as said below
Outputs:
- pruned_weights: bfloat16 [16384, 16384], P('mp', 'dp')
- hessian_rows: float32 [1024, 16384], P('dp', 'mp')
The draws below stay inside these ranges and needn't reach their ends.
Inputs may be any that keep to these rules, and one draw needn't show every extreme that they name: Row r of u_rows is zero left of column r, and its entry in column r is 1 or more. `keep_pairs`: the two positions of a pair differ and the first is the smaller.
All inputs are finite; a program needn't handle non-finite values.
Results may differ from the reference program's by a relative error of at most 0.012.
Values may be sent and summed in bfloat16 or wider, within the bound.
A program may use at most 128 MiB of HBM per device.

```python
import jax
import jax.numpy as jnp
from jax import lax

D = 16384
B = 512
PANELS = 2
WIN = 1024
TOKENS = 16384


def draw_u_rows(key, part):
    base = jax.random.fold_in(key, 7)
    key_diag, key_noise = jax.random.split(base, 2)
    diagonal = jax.random.uniform(key_diag, (WIN, 1), jnp.float32, 1.0, 2.0)
    noise = jax.random.normal(key_noise, (WIN, D), jnp.float32)
    row_index = jnp.arange(WIN, dtype=jnp.int32)[:, None]
    col_index = jnp.arange(D, dtype=jnp.int32)[None, :]
    same_panel = row_index // B == col_index // B
    spread = jnp.where(same_panel, 2.0 / B ** 0.5, 0.05)
    upper = jnp.where(col_index > row_index, noise * spread, 0.0)
    values = upper + jnp.where(col_index == row_index, diagonal, 0.0)
    return values.astype(jnp.float32)


def draw_keep_pairs(key, part):
    picked = jax.random.randint(jax.random.fold_in(key, 11), (PANELS, B // 4), 0, 6)
    firsts = jnp.array([0, 0, 0, 1, 1, 2], jnp.int32)
    seconds = jnp.array([1, 2, 3, 2, 3, 3], jnp.int32)
    onehot = (picked[..., None] == jnp.arange(6, dtype=jnp.int32)).astype(jnp.int32)
    first_pos = jnp.sum(onehot * firsts, axis=-1)
    second_pos = jnp.sum(onehot * seconds, axis=-1)
    return jnp.stack([first_pos, second_pos], axis=-1).astype(jnp.int32)


def steps_of(rng, extent, pieces, least, largest):
    level, own = 1.0, jax.random.fold_in(rng, 6)
    for axis_at, parts in pieces:
        heights = jnp.exp(jax.random.uniform(jax.random.fold_in(own, axis_at), (parts,), jnp.float32, least / len(pieces), largest / len(pieces)))
        level = level * jnp.repeat(heights, extent[axis_at] // parts).reshape([-1 if axis == axis_at else 1 for axis in range(len(extent))])
    return level


def normal_values(own_key, shape, scale, most, pieces=(), kind=jnp.bfloat16):
    entries = jax.random.normal(own_key, shape, jnp.float32) * scale
    if len(pieces) > 0:
        entries = steps_of(own_key, shape, pieces, -0.22, 0.18) * entries
    return jnp.clip(entries, min=-most, max=most).astype(kind)


def setup_inputs(seed: int = 0) -> dict:
    keys = jax.random.split(jax.random.key(seed), 5)
    return {
        "features": normal_values(keys[0], (TOKENS, D), 1.0, 6.0, ((0, 8), (1, 16))),
        "weights": normal_values(keys[1], (D, D), 1.0, 6.0, ((0, 16), (1, 8))),
        "u_rows": draw_u_rows(jax.random.fold_in(keys[4], 71), 0),
        "keep_pairs": draw_keep_pairs(jax.random.fold_in(keys[4], 71), 0),
    }


def keep_columns(pairs):
    positions = jnp.arange(4, dtype=jnp.int32)
    selected = (pairs[:, 0:1] == positions) | (pairs[:, 1:2] == positions)
    return selected.astype(jnp.float32).reshape(-1)

def solve_errors(panel_cols, diag_block, keep):
    pruned = 1.0 - keep
    system = diag_block * pruned[:, None] * pruned[None, :] + jnp.diag(keep)
    return lax.linalg.triangular_solve(system, panel_cols * pruned[None, :], left_side=False, lower=False, transpose_a=False)

def reference(features, weights, u_rows, keep_pairs):
    window = features[:, :WIN]
    gram = lax.dot_general(window.astype(jnp.float32), features.astype(jnp.float32), (((0,), (0,)), ((), ())), preferred_element_type=jnp.float32)
    hessian_rows = gram * (2.0 / TOKENS)
    current = weights.astype(jnp.float32)
    keep_list = [keep_columns(keep_pairs[panel]) for panel in range(PANELS)]
    error_list = []
    for panel in range(PANELS):
        panel_cols = current[:, panel * B:(panel + 1) * B]
        for earlier in range(panel):
            panel_cols = panel_cols - jnp.dot(error_list[earlier], u_rows[earlier * B:(earlier + 1) * B, panel * B:(panel + 1) * B], precision=lax.Precision.HIGHEST)
        diag_block = u_rows[panel * B:(panel + 1) * B, panel * B:(panel + 1) * B]
        error_list.append(solve_errors(panel_cols, diag_block, keep_list[panel]))
    errors = jnp.concatenate(error_list, axis=1)
    updated = current - jnp.dot(errors, u_rows, precision=lax.Precision.HIGHEST)
    column_mask = jnp.concatenate(keep_list + [jnp.ones((D - WIN,), jnp.float32)])
    pruned_weights = (updated * column_mask[None, :]).astype(jnp.bfloat16)
    return (pruned_weights, hessian_rows)
```

```python
import jax
import jax.numpy as jnp
from jax import lax
from jax.experimental import pallas as pl
from jax.experimental.pallas import tpu as pltpu
from jax.sharding import PartitionSpec as P

B = 512
PANELS = 2
WIN = 1024
TOKENS = 16384
HALF = WIN // 2
CORNER = HALF
LOCAL_COLS = 2048
GATHER_COLS = CORNER + LOCAL_COLS
STEPS = 16
PAIR_OFFSETS = (2, 1, 3, 0)
CROSS_AT = (3, 2, 1, 0)
MESH = pl.DeviceIdType.MESH
EXACT = lax.Precision.HIGHEST


def pruned_positions(keep_pairs):
    first, second = keep_pairs[..., 0], keep_pairs[..., 1]
    low = jnp.where(first != 0, 0, jnp.where(second != 1, 1, 2))
    high = jnp.where(second != 3, 3, jnp.where(first != 2, 2, 1))
    both = jnp.stack([low, high], axis=-1).reshape(WIN // 4, 2)
    return (both + 4 * jnp.arange(WIN // 4, dtype=jnp.int32)[:, None]).reshape(HALF)


def keep_columns(pairs):
    positions = jnp.arange(4, dtype=jnp.int32)
    selected = (pairs[:, 0:1] == positions) | (pairs[:, 1:2] == positions)
    return selected.astype(jnp.float32).reshape(-1)


def iota(shape, dim):
    return lax.broadcasted_iota(jnp.int32, shape, dim)


def kernel(
    feat_hbm, w_hbm, u_hbm, lane_idx, row_idx, mask_ref, out_hbm, hess_hbm,
    feat, feat_t, win, acc, sums, relay, from_left, from_right, from_pair,
    wv, uv, ug, wcs, wcb, ev, tri, inv, hout,
    local_sem, win_sem, send_sem, recv_sem,
):
    dp, mp = lax.axis_index("dp"), lax.axis_index("mp")
    x, l = lax.div(dp, 2), lax.rem(dp, 2)
    z, h, k = lax.div(mp, 4), lax.rem(lax.div(mp, 2), 2), lax.rem(mp, 2)
    way = 1 - 2 * k
    r = lax.rem(z * way + 4, 4)
    is_source = mp == 0
    is_owner = dp == 0

    def at_mp(zz, hh, kk):
        return (dp, lax.rem(zz + 8, 4) * 4 + hh * 2 + kk)

    def at_dp(xx, ll):
        return (lax.rem(xx + 8, 4) * 2 + ll, mp)

    pending = []
    count = {"send": 0, "recv": 0}

    def take(kind):
        count[kind] += 1
        return count[kind] - 1

    def remote(src, dst, sent, landed, device):
        return pltpu.make_async_remote_copy(
            src_ref=src, dst_ref=dst, send_sem=send_sem.at[sent], recv_sem=recv_sem.at[landed],
            device_id=device, device_id_type=MESH,
        )

    def guarded(when, run):
        if when is None:
            run()
        else:
            pl.when(when)(run)

    def send(src, dst, landed, device, when=None):
        sent = take("send")
        guarded(when, lambda: remote(src, dst, sent, landed, device).start())
        pending.append((when, src, dst, sent, landed, device))

    def arrived(dst, landed, when=None):
        guarded(when, lambda: remote(dst, dst, 0, landed, at_mp(z, h, 1 - k)).wait_recv())

    load_u = pltpu.make_async_copy(u_hbm, uv, local_sem.at[0])
    load_f = pltpu.make_async_copy(feat_hbm, feat, local_sem.at[1])
    load_w = pltpu.make_async_copy(w_hbm, wv, local_sem.at[2])
    load_u.start()

    def window_block(i):
        t, tq = divmod(i, 4)
        column = pl.multiple_of(lax.rem(x + PAIR_OFFSETS[t], 4) * 256, 256)
        return pltpu.make_async_copy(
            feat_hbm.at[pl.ds(tq * 512, 512), pl.ds(column, 256)], win.at[t, tq], win_sem.at[i]
        )

    @pl.when(is_source)
    def _():
        for i in range(STEPS):
            window_block(i).start()

    load_f.start()
    load_w.start()

    barrier = pltpu.get_barrier_semaphore()
    peers = [(lax.rem(dp + o, 8), mp) for o in range(1, 8)]
    peers += [at_mp(z + 1, h, k), at_mp(z - 1, h, k), at_mp(z, 1 - h, k), at_mp(z, h, 1 - k)]
    for peer in peers:
        pl.semaphore_signal(barrier, inc=1, device_id=peer, device_id_type=MESH)

    load_u.wait()
    picked_rows = (iota((32, 64), 1) + 64 * mp) == row_idx[pl.ds(pl.multiple_of(mp * 32, 32), 32), :]
    picked = jnp.dot(
        picked_rows.astype(jnp.bfloat16), uv[...].astype(jnp.bfloat16), preferred_element_type=jnp.float32
    ).astype(jnp.bfloat16)
    ug[z, h, k, :, CORNER:] = picked

    def column_pick(c):
        wanted = lane_idx[:, c * 128 : (c + 1) * 128]
        return ((iota((256, 128), 0) + 256 * c) == wanted).astype(jnp.bfloat16)

    @pl.when(is_owner)
    def _():
        for c in range(4):
            ug[z, h, k, :, c * 128 : (c + 1) * 128] = jnp.dot(
                picked[:, c * 256 : (c + 1) * 256], column_pick(c), preferred_element_type=jnp.float32
            ).astype(jnp.bfloat16)

    pl.semaphore_wait(barrier, len(peers))

    own_landed = [take("recv") for _ in range(STEPS)]
    partner_landed = [take("recv") for _ in range(STEPS)]

    def piece(i, half):
        t, tq = divmod(i, 4)
        return win.at[t, tq, :, pl.ds(pl.multiple_of(half * 128, 128), 128)]

    def relay_piece(i):
        q = CROSS_AT[i // 4]

        @pl.when(is_source)
        def _():
            window_block(i).wait()

        own = piece(i, k)
        arrived(own, own_landed[i], when=jnp.logical_not(is_source))
        on_first = h == 0
        forward = (on_first & (r < 3)) | ((h == 1) & ((r == q) | (r == (q + 1) % 4)))
        send(own, own, own_landed[i], at_mp(z + way, h, k), when=forward)
        send(own, own, own_landed[i], at_mp(z, 1, k), when=on_first & (r == q))
        send(own, own, own_landed[i], at_mp(z - way, h, k), when=(h == 1) & (r == q))
        other = piece(i, 1 - k)
        send(other, other, own_landed[i], at_mp(z, h, 1 - k), when=is_source)
        send(own, own, partner_landed[i], at_mp(z, h, 1 - k), when=mp != 1)
        return lambda: arrived(other, partner_landed[i], when=jnp.logical_not(is_source))

    corner_landed = take("recv")
    corner = ug.at[z, h, k, :, pl.ds(0, CORNER)]
    for o in range(1, 8):
        send(corner, corner, corner_landed, (lax.rem(dp + o, 8), mp), when=is_owner)

    part_landed = take("recv")
    load_w.wait()

    @pl.when(is_owner)
    def _():
        for c in range(4):
            wcs[:, c * 128 : (c + 1) * 128] = jnp.dot(
                wv[:, c * 256 : (c + 1) * 256], column_pick(c), preferred_element_type=jnp.float32
            ).astype(jnp.bfloat16)
        wcb[0, 0] = wcs[0:128, :]

    for o in range(1, 8):
        send(
            wcs.at[pl.ds(o * 128, 128), :], wcb.at[o // 2, o % 2], part_landed, (jnp.int32(o), mp), when=is_owner
        )

    load_f.wait()

    @pl.loop(0, 8)
    def _(tb):
        block = feat[pl.ds(pl.multiple_of(tb * 256, 256), 256), :]
        feat_t[lax.div(tb, 2), :, pl.ds(pl.multiple_of(lax.rem(tb, 2) * 256, 256), 256)] = block.T

    arrived(corner, corner_landed, when=jnp.logical_not(is_owner))

    class Gather:
        def __init__(self, view, both, pos, line, device):
            self.view, self.both, self.pos, self.line, self.device = view, both, pos, line, device
            self.landed = [take("recv") for _ in range(5)]
            self.after = lax.rem(pos + 1, 4)
            self.before = lax.rem(pos + 3, 4)
            self.far = lax.rem(pos + 2, 4)

        def first(self):
            own = self.view(self.pos, self.line)
            send(own, own, self.landed[0], self.device(self.pos, 1 - self.line))

        def second(self):
            arrived(self.view(self.pos, 1 - self.line), self.landed[0])
            own = self.both(self.pos)
            send(own, own, self.landed[1], self.device(self.pos + 1, self.line))
            send(own, own, self.landed[2], self.device(self.pos - 1, self.line))

        def third(self):
            arrived(self.both(self.before), self.landed[1])
            arrived(self.both(self.after), self.landed[2])
            up, down = self.view(self.before, 0), self.view(self.after, 1)
            send(up, up, self.landed[3], self.device(self.pos + 1, self.line))
            send(down, down, self.landed[4], self.device(self.pos - 1, self.line))

        def finish(self):
            arrived(self.view(self.far, 0), self.landed[3])
            arrived(self.view(self.far, 1), self.landed[4])

    u_gather = Gather(
        lambda p, q: ug.at[p, q, k], lambda p: ug.at[p, :, k], z, h, lambda p, q: at_mp(p, q, k)
    )
    w_gather = Gather(lambda p, q: wcb.at[p, q], lambda p: wcb.at[p], x, l, at_dp)
    plane_landed = take("recv")

    def finish_u():
        u_gather.finish()
        plane = ug.at[:, :, k]
        send(plane, plane, plane_landed, at_mp(z, h, 1 - k))

    def start_w():
        arrived(wcb.at[x, l], part_landed, when=jnp.logical_not(is_owner))
        w_gather.first()

    u_gather.first()
    hooks = {
        2: u_gather.second, 6: u_gather.third, 11: finish_u,
        4: start_w, 7: w_gather.second, 10: w_gather.third, 14: w_gather.finish,
    }

    relay_landed, left_landed, right_landed, pair_landed = (take("recv") for _ in range(4))

    def add_to_acc(source):
        @pl.loop(0, 4)
        def _(m):
            rows = pl.ds(pl.multiple_of(m * 256, 256), 256)
            acc[rows, :] += source[rows, :].astype(jnp.float32)

    def round_acc(slot):
        @pl.loop(0, 4)
        def _(m):
            rows = pl.ds(pl.multiple_of(m * 256, 256), 256)
            sums[slot, rows, :] = acc[rows, :].astype(jnp.bfloat16)

    def reduce_pair(t):
        if t == 0:
            round_acc(0)
            send(sums.at[0], relay, relay_landed, at_dp(x + way, l))
        elif t == 1:
            @pl.when(k == 0)
            def _():
                arrived(relay, relay_landed)
                add_to_acc(relay)

            round_acc(1)
            send(sums.at[1], from_left, left_landed, at_dp(x + 1, l))
        elif t == 2:
            @pl.when(k == 1)
            def _():
                arrived(relay, relay_landed)
                add_to_acc(relay)

            round_acc(2)
            send(sums.at[2], from_right, right_landed, at_dp(x - 1, l))
        else:
            arrived(from_left, left_landed)
            arrived(from_right, right_landed)
            add_to_acc(from_left)
            add_to_acc(from_right)
            mine = pl.ds(pl.multiple_of(l * 128, 128), 128)
            theirs = pl.ds(pl.multiple_of((1 - l) * 128, 128), 128)
            sums[3, :, 0:128] = acc[:, theirs].astype(jnp.bfloat16)
            send(sums.at[3, :, pl.ds(0, 128)], from_pair, pair_landed, at_dp(x, 1 - l))
            return mine

    for i in range(STEPS):
        t, tq = divmod(i, 4)
        partner_here = relay_piece(i)
        if i in hooks:
            hooks[i]()
        partner_here()

        @pl.loop(0, 2)
        def _(m):
            rows = pl.ds(pl.multiple_of(m * 512, 512), 512)
            product = jnp.dot(feat_t[tq, rows, :], win[t, tq], preferred_element_type=jnp.float32)
            if tq == 0:
                acc[rows, :] = product
            else:
                acc[rows, :] += product

        if tq == 3:
            mine = reduce_pair(t)

    arrived(ug.at[:, :, 1 - k], plane_landed)
    tri[...] = ug[:, :, :, :, 0:CORNER].reshape(HALF, CORNER).astype(jnp.float32)
    row, col = iota((128, 128), 0), iota((128, 128), 1)
    inverses = []
    for j in range(4):
        block = tri[j * 128 : (j + 1) * 128, j * 128 : (j + 1) * 128]
        inverses.append(jnp.where(row == col, 1.0 / jnp.where(row == col, block, 1.0), 0.0))
    for level in range(7):
        for j in range(4):
            block = tri[j * 128 : (j + 1) * 128, j * 128 : (j + 1) * 128]
            upper_part = ((row >> level) + 1 == (col >> level)) & ((row >> (level + 1)) == (col >> (level + 1)))
            step = jnp.dot(jnp.where(upper_part, block, 0.0), inverses[j], precision=EXACT)
            inverses[j] = inverses[j] - jnp.dot(inverses[j], step, precision=EXACT)
    for j in range(4):
        inv[j] = inverses[j]

    @pl.loop(0, 8)
    def _(m):
        solved = []
        for j in range(4):
            rest = wcb[lax.div(m, 2), lax.rem(m, 2), :, j * 128 : (j + 1) * 128].astype(jnp.float32)
            for e in range(j):
                rest -= jnp.dot(
                    solved[e], tri[e * 128 : (e + 1) * 128, j * 128 : (j + 1) * 128], precision=EXACT
                )
            solved.append(jnp.dot(rest, inv[j], precision=EXACT))
            ev[pl.ds(pl.multiple_of(m * 128, 128), 128), j * 128 : (j + 1) * 128] = solved[j].astype(jnp.bfloat16)

    @pl.loop(0, 8)
    def _(c):
        cols = pl.ds(pl.multiple_of(c * 256, 256), 256)
        factor = ug[:, :, :, :, pl.ds(pl.multiple_of(c * 256 + CORNER, 256), 256)].reshape(HALF, 256)
        change = jnp.dot(ev[...], factor, preferred_element_type=jnp.float32)
        wv[:, cols] = ((wv[:, cols].astype(jnp.float32) - change) * mask_ref[:, cols]).astype(jnp.bfloat16)

    store_w = pltpu.make_async_copy(wv, out_hbm, local_sem.at[0])
    store_w.start()

    arrived(from_pair, pair_landed)
    total = (acc[:, mine] + from_pair[...].astype(jnp.float32)) * (2.0 / TOKENS)
    hout[...] = total.T
    store_h = pltpu.make_async_copy(hout, hess_hbm, local_sem.at[1])
    store_h.start()

    for when, src, dst, sent, landed, device in pending:
        guarded(when, lambda: remote(src, dst, sent, landed, device).wait_send())
    store_w.wait()
    store_h.wait()


def body(features, weights, u_rows, keep_pairs):
    pruned = pruned_positions(keep_pairs)
    keep = jnp.concatenate([keep_columns(keep_pairs[panel]) for panel in range(PANELS)])
    mask = jnp.concatenate([keep, jnp.ones((LOCAL_COLS - WIN,), jnp.float32)])
    mask = jnp.where(lax.axis_index("dp") == 0, mask, 1.0)[None, :]
    bf16, f32 = jnp.bfloat16, jnp.float32
    anywhere = pl.BlockSpec(memory_space=pl.ANY)
    vmem = pl.BlockSpec(memory_space=pltpu.VMEM)
    return pl.pallas_call(
        kernel,
        out_shape=(
            jax.ShapeDtypeStruct((1024, LOCAL_COLS), bf16),
            jax.ShapeDtypeStruct((128, 1024), f32),
        ),
        in_specs=[anywhere, anywhere, anywhere, vmem, vmem, vmem],
        out_specs=(anywhere, anywhere),
        scratch_shapes=[
            pltpu.VMEM((2048, 1024), bf16),
            pltpu.VMEM((4, 1024, 512), bf16),
            pltpu.VMEM((4, 4, 512, 256), bf16),
            pltpu.VMEM((1024, 256), f32),
            pltpu.VMEM((4, 1024, 256), bf16),
            pltpu.VMEM((1024, 256), bf16),
            pltpu.VMEM((1024, 256), bf16),
            pltpu.VMEM((1024, 256), bf16),
            pltpu.VMEM((1024, 128), bf16),
            pltpu.VMEM((1024, LOCAL_COLS), bf16),
            pltpu.VMEM((64, LOCAL_COLS), f32),
            pltpu.VMEM((4, 2, 2, 32, GATHER_COLS), bf16),
            pltpu.VMEM((1024, HALF), bf16),
            pltpu.VMEM((4, 2, 128, HALF), bf16),
            pltpu.VMEM((1024, HALF), bf16),
            pltpu.VMEM((HALF, HALF), f32),
            pltpu.VMEM((4, 128, 128), f32),
            pltpu.VMEM((128, 1024), f32),
            pltpu.SemaphoreType.DMA((3,)),
            pltpu.SemaphoreType.DMA((STEPS,)),
            pltpu.SemaphoreType.DMA((128,)),
            pltpu.SemaphoreType.DMA((64,)),
        ],
        compiler_params=pltpu.CompilerParams(
            collective_id=0, has_side_effects=True, vmem_limit_bytes=60 * 1024 * 1024
        ),
    )(features, weights, u_rows, pruned[None, :], pruned[:, None], mask)


def solution(mesh):
    in_specs = (P("dp", "mp"), P("mp", "dp"), P("mp", "dp"), P())
    out_specs = (P("mp", "dp"), P("dp", "mp"))
    return jax.shard_map(body, mesh=mesh, in_specs=in_specs, out_specs=out_specs, check_vma=False)
```

```python
import jax
import jax.numpy as jnp
from jax import lax
from jax.experimental import pallas as pl
from jax.experimental.pallas import tpu as pltpu
from jax.sharding import PartitionSpec as P

B = 512
PANELS = 2
WIN = 1024
TOKENS = 16384
HALF = WIN // 2
CORNER = HALF
LOCAL_COLS = 2048
STEPS = 16
LAG = 3
PAIR_OFFSETS = (2, 1, 3, 0)
MESH = pl.DeviceIdType.MESH
EXACT = lax.Precision.HIGHEST


def iota(shape, dim):
    return lax.broadcasted_iota(jnp.int32, shape, dim)


def pruned_of(first, second):
    low = jnp.where(first != 0, 0, jnp.where(second != 1, 1, 2))
    high = jnp.where(second != 3, 3, jnp.where(first != 2, 2, 1))
    return low, high


def pruned_lanes(low, high):
    groups = low.shape[0]
    shape = (groups, 2 * groups)
    group, lane = iota(shape, 0), iota(shape, 1)
    own = jnp.where((lane & 1) == 0, low, high) + 4 * group
    return jnp.sum(jnp.where((lane >> 1) == group, own, 0), axis=0, keepdims=True)


def kept_lanes(low, high):
    groups = low.shape[0]
    shape = (groups, 4 * groups)
    group, lane = iota(shape, 0), iota(shape, 1)
    pruned = ((lane >> 2) == group) & (((lane & 3) == low) | ((lane & 3) == high))
    return 1.0 - jnp.sum(jnp.where(pruned, 1.0, 0.0), axis=0, keepdims=True)


def kernel(
    feat_hbm, w_hbm, u_hbm, pairs_ref, out_hbm, hess_hbm,
    feat, feat_t, win, acc, sums, to_pair, relay, from_left, from_right, from_pair,
    wv, uv, picked_rows, ug, cg, wcs, wcb, ev, parts, halves, inv, mask, picks, low_high, hout,
    local_sem, win_sem, send_sem, recv_sem,
):
    dp, mp = lax.axis_index("dp"), lax.axis_index("mp")
    x, l = lax.div(dp, 2), lax.rem(dp, 2)
    z, h, k = lax.div(mp, 4), lax.rem(lax.div(mp, 2), 2), lax.rem(mp, 2)
    is_source = mp == 0
    is_owner = dp == 0
    f32, bf16 = jnp.float32, jnp.bfloat16

    def at_mp(zz, hh, kk):
        return (dp, lax.rem(zz + 8, 4) * 4 + hh * 2 + kk)

    def at_dp(xx, ll):
        return (lax.rem(xx + 8, 4) * 2 + ll, mp)

    counter = [0]

    def take(n=1):
        counter[0] += n
        return counter[0] - n

    piece_landed = take(2 * STEPS)
    shared_landed = take(2 * STEPS)
    u_landed, c_landed, w_landed = take(5), take(5), take(5)
    picked_landed, corner_landed, part_landed = take(1), take(2), take(2)
    level_landed, inverse_landed, rows_landed = take(4), take(1), take(1)
    relay_landed, left_landed, right_landed, pair_landed = take(1), take(1), take(1), take(1)

    def remote(src, dst, sent, landed, device):
        return pltpu.make_async_remote_copy(
            src_ref=src, dst_ref=dst, send_sem=send_sem.at[sent], recv_sem=recv_sem.at[landed],
            device_id=device, device_id_type=MESH,
        )

    def arrived(dst, landed):
        remote(dst, dst, 0, landed, at_mp(z, h, 1 - k)).wait_recv()

    load_u = pltpu.make_async_copy(u_hbm, uv, local_sem.at[0])
    load_f = pltpu.make_async_copy(feat_hbm, feat, local_sem.at[1])
    load_w = pltpu.make_async_copy(w_hbm, wv, local_sem.at[2])
    load_u.start()

    def window_block(i, half):
        t, tq = divmod(i, 4)
        column = pl.multiple_of(lax.rem(x + PAIR_OFFSETS[t], 4) * 256 + half * 128, 128)
        return pltpu.make_async_copy(
            feat_hbm.at[pl.ds(tq * 512, 512), pl.ds(column, 128)], win.at[t, tq, half], win_sem.at[2 * i + half]
        )

    @pl.when(is_source)
    def _():
        for i in range(STEPS):
            for half in range(2):
                window_block(i, half).start()

    load_w.start()
    load_f.start()

    barrier = pltpu.get_barrier_semaphore()
    peers = [(lax.rem(dp + o, 8), mp) for o in range(1, 8)]
    peers += [(lax.rem(dp + o, 8), mp + 1 - 2 * k) for o in range(1, 8)]
    peers += [at_mp(z + 1, h, k), at_mp(z - 1, h, k), at_mp(z, 1 - h, k), at_mp(z, h, 1 - k)]
    for peer in peers:
        pl.semaphore_signal(barrier, inc=1, device_id=peer, device_id_type=MESH)

    wide = jnp.concatenate([pairs_ref[0], pairs_ref[1], pairs_ref[0], pairs_ref[1]], axis=0).astype(f32)
    tall = wide.T.astype(jnp.int32)
    for panel in range(PANELS):
        low, high = pruned_of(tall[:, 2 * panel : 2 * panel + 1], tall[:, 2 * panel + 1 : 2 * panel + 2])
        low_high[0, panel * 128 : (panel + 1) * 128, :] = low
        low_high[1, panel * 128 : (panel + 1) * 128, :] = high
    for c in range(4):
        low, high = low_high[0, c * 64 : (c + 1) * 64, :], low_high[1, c * 64 : (c + 1) * 64, :]
        picks[c] = (iota((256, 128), 0) == pruned_lanes(low, high)).astype(bf16)
        mask[:, c * 256 : (c + 1) * 256] = jnp.where(is_owner, kept_lanes(low, high), 1.0)

    own_groups = pl.ds(pl.multiple_of(mp * 16, 16), 16)
    own_rows = pruned_lanes(low_high[0, own_groups, :], low_high[1, own_groups, :])
    row_pick = (iota((64, 32), 0) == own_rows).astype(bf16)
    load_u.wait()
    picked = lax.dot_general(
        row_pick, uv[...].astype(bf16), (((0,), (0,)), ((), ())), preferred_element_type=f32
    ).astype(bf16)
    picked_rows[...] = picked

    @pl.when(k == 1)
    def _():
        ug[z, h, 1] = picked


    @pl.when(is_owner)
    def _():
        for c in range(4):
            cg[z, h, k, :, c * 128 : (c + 1) * 128] = jnp.dot(
                picked[:, c * 256 : (c + 1) * 256], picks[c], preferred_element_type=f32
            ).astype(bf16)

    pl.semaphore_wait(barrier, len(peers))

    def pick_weights():
        load_w.wait()

        @pl.when(is_owner)
        def _():
            for c in range(4):
                wcs[:, c * 128 : (c + 1) * 128] = jnp.dot(
                    wv[:, c * 256 : (c + 1) * 256], picks[c], preferred_element_type=f32
                ).astype(bf16)

    def transpose_features():
        load_f.wait()

        @pl.loop(0, 8)
        def _(tb):
            block = feat[pl.ds(pl.multiple_of(tb * 256, 256), 256), :]
            feat_t[lax.div(tb, 2), :, pl.ds(pl.multiple_of(lax.rem(tb, 2) * 256, 256), 256)] = block.T

    def product(i):
        t, tq = divmod(i, 4)

        @pl.loop(0, 2)
        def _(m):
            rows = pl.ds(pl.multiple_of(m * 512, 512), 512)
            columns = jnp.concatenate([win[t, tq, 0], win[t, tq, 1]], axis=1)
            part = jnp.dot(feat_t[tq, rows, :], columns, preferred_element_type=f32)
            if tq == 0:
                acc[t, rows, :] = part
            else:
                acc[t, rows, :] += part

    def add_to(slot, source):
        @pl.loop(0, 4)
        def _(m):
            rows = pl.ds(pl.multiple_of(m * 256, 256), 256)
            acc[slot, rows, :] += source[rows, :].astype(f32)

    def round_sum(slot):
        @pl.loop(0, 4)
        def _(m):
            rows = pl.ds(pl.multiple_of(m * 256, 256), 256)
            sums[slot, rows, :] = acc[slot, rows, :].astype(bf16)

    mine = pl.ds(pl.multiple_of(l * 128, 128), 128)
    theirs = pl.ds(pl.multiple_of((1 - l) * 128, 128), 128)

    def update_columns(c):
        cols = pl.ds(c * 256, 256)
        factor = ug[:, :, :, :, cols].reshape(HALF, 256)
        updated = wv[:, cols].astype(f32) - jnp.dot(ev[...], factor, preferred_element_type=f32)
        if c < 4:
            updated = updated * mask[:, c * 256 : (c + 1) * 256]
        wv[:, cols] = updated.astype(bf16)

    def solve_rows(core):
        @pl.loop(0, 2)
        def _(m):
            lead = wcb[pl.ds(m * 2, 2), :, core].reshape(512, HALF)
            rows = pl.ds(pl.multiple_of(m * 512, 512), 512)
            first = lead[:, 0:256]
            ev[rows, 0:256] = (
                jnp.dot(first, inv[0, 0:256, 0:256], preferred_element_type=f32)
                + jnp.dot(first, inv[1, 0:256, 0:256], preferred_element_type=f32)
            ).astype(bf16)
            ev[rows, 256:] = (
                jnp.dot(lead, inv[0, :, 256:], preferred_element_type=f32)
                + jnp.dot(lead, inv[1, :, 256:], preferred_element_type=f32)
            ).astype(bf16)

    store_w = pltpu.make_async_copy(wv, out_hbm, local_sem.at[0])
    store_h = pltpu.make_async_copy(hout, hess_hbm, local_sem.at[1])

    def run(core):
        way = 1 - 2 * core
        pending = []
        sends = [0]
        partner = at_mp(z, h, 1 - core)

        def send(src, dst, landed, device, when=None):
            sent = sends[0]
            sends[0] += 1
            make = lambda: remote(src, dst, sent, landed, device)
            if when is None:
                make().start()
            else:
                pl.when(when)(lambda: make().start())
            pending.append((when, make))

        def send_right(do_round=True):
            round_sum(1)
            send(sums.at[1], from_left, left_landed, at_dp(x + 1, l))

        def send_left():
            round_sum(2)
            send(sums.at[2], from_right, right_landed, at_dp(x - 1, l))

        def add_relayed(slot):
            arrived(relay, relay_landed)
            add_to(slot, relay)

        def reduce_pairs(i):
            if i == 3:
                round_sum(0)
                send(sums.at[0], relay, relay_landed, at_dp(x + way, l))
            if core == 0:
                if i == 9:
                    add_relayed(1)
                    send_right()
                if i == 11:
                    send_left()
            else:
                if i == 7:
                    send_right()
                if i == 11:
                    add_relayed(2)
                    send_left()

        def reduce_own():
            arrived(from_left, left_landed)
            arrived(from_right, right_landed)
            add_to(3, from_left)
            add_to(3, from_right)
            to_pair[...] = acc[3, :, theirs].astype(bf16)
            send(to_pair, from_pair, pair_landed, at_dp(x, 1 - l))

        def finish_hessian():
            arrived(from_pair, pair_landed)
            total = (acc[3, :, mine] + from_pair[...].astype(f32)) * (2.0 / TOKENS)
            hout[...] = total.T
            store_h.start()

        def send_corner():
            for o in range(7, -1, -1):
                device = (jnp.int32(o), mp + 1 - core)
                if o == 0:
                    if core == 0:
                        send(cg.at[z, h, 0], cg.at[z, h, 0], corner_landed, device, when=is_owner)
                else:
                    send(cg.at[z, h, core], cg.at[z, h, core], corner_landed + core, device, when=is_owner)

        def send_weights():
            pick_weights()
            for o in range(7, -1, -1):
                device = (jnp.int32(o), mp + 1 - core)
                part = wcs.at[pl.ds(o * 128, 128), :]
                target = wcb.at[o // 2, o % 2, core]
                if o == 0:
                    if core == 0:
                        send(part, target, part_landed, device, when=is_owner)
                else:
                    send(part, target, part_landed + core, device, when=is_owner)

        if core == 0:
            late = jnp.where((z == 1) | (z == 3), LAG, 0)
            early_set = jnp.where(z == 3, 1, 0)
            send_base = 0

            def piece(i, half):
                return win.at[lax.div(i, 4), lax.rem(i, 4), half]

            def routes(half):
                step = 1 - 2 * half
                r = lax.rem(z * step + 4, 4)
                on_first = h == 0
                forward = (on_first & (r < 3)) | ((h == 1) & ((r == 1) | (r == 2)))
                cross = on_first & (r == 1)
                back = (h == 1) & (r == 1)
                return (
                    (forward, at_mp(z + step, h, 0), 0),
                    (cross, at_mp(z, 1, 0), 1),
                    (back, at_mp(z - step, h, 0), 2),
                )

            def copies(i, half):
                ref = piece(i, half)
                slot = 2 * i + half
                for when, device, kind in routes(half):
                    yield when, remote(ref, ref, 4 * slot + kind, piece_landed + slot, device)
                yield None, remote(ref, ref, 4 * slot + 3, shared_landed + slot, partner)

            def pass_on(i, half):
                for when, copy in copies(i, half):
                    if when is None:
                        copy.start()
                    else:
                        pl.when(when)(copy.start)

            sends[0] = 8 * STEPS

            def start_pieces(some):
                @pl.when(is_source)
                def _():
                    for i in some:
                        for half in range(2):
                            window_block(i, half).wait()
                            pass_on(i, half)

            send_corner()
            send(picked_rows, ug.at[z, h, 0], picked_landed, partner)
            start_pieces(range(4))
            send_weights()
            start_pieces(range(4, STEPS))
            transpose_features()

            def take_piece(i, half):
                arrived(piece(i, half), piece_landed + 2 * i + half)
                pass_on(i, half)

            for step in range(STEPS + LAG):
                if step < STEPS:
                    pl.when(jnp.logical_not(is_source))(lambda: take_piece(step, early_set))
                index = step - late
                ready = jnp.logical_not(is_source) & (index >= 0) & (index < STEPS)
                pl.when(ready)(lambda: take_piece(index, 1 - early_set))
                i = step - LAG
                if i >= 0:
                    product(i)
                    reduce_pairs(i)

            reduce_own()
            arrived(inv, inverse_landed)
            arrived(wcb.at[:, :, 0], rows_landed)
            solve_rows(0)
            for n, zz in enumerate((z, z + 3, z + 1, z + 2)):
                arrived(ug.at[lax.rem(zz, 4)], level_landed + n)
            for c in range(8):
                update_columns(c)
            store_w.start()
            finish_hessian()
            for i in range(STEPS):
                for half in range(2):
                    for when, copy in copies(jnp.int32(i), half):
                        if when is None:
                            copy.wait_send()
                        else:
                            pl.when(when)(copy.wait_send)
        else:

            class Gather:
                def __init__(self, buffer, landed, pos, line, device):
                    self.buffer, self.pos, self.line, self.device = buffer, pos, line, device
                    self.landed = landed
                    self.after = lax.rem(pos + 1, 4)
                    self.before = lax.rem(pos + 3, 4)
                    self.far = lax.rem(pos + 2, 4)

                def move(self, view, n, device):
                    send(view, view, self.landed + n, device)

                def first(self):
                    self.move(self.buffer.at[self.pos, self.line], 0, self.device(self.pos, 1 - self.line))

                def second(self):
                    arrived(self.buffer.at[self.pos, 1 - self.line], self.landed)
                    own = self.buffer.at[self.pos]
                    self.move(own, 1, self.device(self.pos + 1, self.line))
                    self.move(own, 2, self.device(self.pos - 1, self.line))

                def third(self):
                    arrived(self.buffer.at[self.before], self.landed + 1)
                    arrived(self.buffer.at[self.after], self.landed + 2)
                    self.move(self.buffer.at[self.before, 0], 3, self.device(self.pos + 1, self.line))
                    self.move(self.buffer.at[self.after, 1], 4, self.device(self.pos - 1, self.line))

                def finish(self):
                    arrived(self.buffer.at[self.far, 0], self.landed + 3)
                    arrived(self.buffer.at[self.far, 1], self.landed + 4)

            over_mp = lambda p, q: at_mp(p, q, 1)
            u_gather = Gather(ug, u_landed, z, h, over_mp)
            c_gather = Gather(cg, c_landed, z, h, over_mp)
            w_gather = Gather(wcb, w_landed, x, l, at_dp)
            levels = (u_gather.pos, u_gather.before, u_gather.after, u_gather.far)

            def share_level(n):
                send(ug.at[levels[n]], ug.at[levels[n]], level_landed + n, partner)

            row, col = iota((128, 128), 0), iota((128, 128), 1)

            def system(i, j, rows, cols):
                view = cg[i : i + rows // 128, :, :, :, j * 128 : j * 128 + cols]
                return view.reshape(rows, cols).astype(f32)

            def exact_dot(a, b):
                return jnp.dot(a, b, precision=EXACT)

            def invert_diagonal():
                for j in range(4):
                    block = system(j, j, 128, 128)
                    parts[j] = jnp.where(row == col, 1.0 / jnp.where(row == col, block, 1.0), 0.0)

            def invert_level(level):
                same = (row >> (level + 1)) == (col >> (level + 1))
                upper_part = ((row >> level) + 1 == (col >> level)) & same
                steps = [exact_dot(jnp.where(upper_part, system(j, j, 128, 128), 0.0), parts[j]) for j in range(4)]
                for j in range(4):
                    parts[j] = parts[j] - exact_dot(parts[j], steps[j])

            def invert_halves():
                for j in range(2):
                    low, high = parts[2 * j], parts[2 * j + 1]
                    halves[j, 0:128, 0:128] = low
                    halves[j, 128:, 128:] = high
                    halves[j, 128:, 0:128] = jnp.zeros((128, 128), f32)
                    halves[j, 0:128, 128:] = -exact_dot(low, exact_dot(system(2 * j, 2 * j + 1, 128, 128), high))

            def keep_split(part, rows, cols):
                rounded = part.astype(bf16)
                inv[0, rows : rows + 256, cols : cols + 256] = rounded
                inv[1, rows : rows + 256, cols : cols + 256] = (part - rounded.astype(f32)).astype(bf16)

            def invert_whole():
                keep_split(halves[0], 0, 0)
                keep_split(halves[1], 256, 256)
                keep_split(-exact_dot(halves[0], exact_dot(system(0, 2, 256, 256), halves[1])), 0, 256)
                for n in range(2):
                    inv[n, 256:, 0:256] = jnp.zeros((256, 256), bf16)
                send(inv, inv, inverse_landed, partner)

            def consume(i):
                for half in range(2):
                    arrived(win.at[i // 4, i % 4, half], shared_landed + 2 * i + half)
                product(i)
                reduce_pairs(i)

            def start_u():
                arrived(ug.at[z, h, 0], picked_landed)
                u_gather.first()

            def start_c():
                arrived(cg.at[z, h, 0], corner_landed)
                pl.when(jnp.logical_not(is_owner))(lambda: arrived(cg.at[z, h, 1], corner_landed + 1))
                c_gather.first()

            def start_w():
                @pl.when(is_owner)
                def _():
                    wcb[0, 0, 1] = wcs[0:128, :]

                arrived(wcb.at[x, l, 0], part_landed)
                pl.when(jnp.logical_not(is_owner))(lambda: arrived(wcb.at[x, l, 1], part_landed + 1))
                w_gather.first()

            def third_u():
                u_gather.third()
                for n in range(3):
                    share_level(n)

            def finish_u():
                u_gather.finish()
                share_level(3)

            def finish_w():
                w_gather.finish()
                send(wcb.at[:, :, 0], wcb.at[:, :, 0], rows_landed, partner)

            send_corner()
            start_u()
            send_weights()
            start_c()
            transpose_features()
            c_gather.second()
            c_gather.third()
            u_gather.second()
            start_w()
            c_gather.finish()
            invert_diagonal()
            for n in range(3):
                invert_level(n)
            w_gather.second()
            for n in range(3, 7):
                invert_level(n)
            invert_halves()
            invert_whole()
            third_u()
            consume(0)
            consume(1)
            w_gather.third()
            consume(2)
            consume(3)
            finish_u()
            consume(4)
            consume(5)
            finish_w()
            consume(6)
            consume(7)
            solve_rows(1)
            for i in range(8, STEPS):
                update_columns(i - 8)
                consume(i)
            store_w.start()
            reduce_own()
            finish_hessian()

        for when, make in pending:
            if when is None:
                make().wait_send()
            else:
                pl.when(when)(lambda: make().wait_send())
        store_w.wait()
        store_h.wait()

    pl.when(k == 0)(lambda: run(0))
    pl.when(k == 1)(lambda: run(1))


def body(features, weights, u_rows, keep_pairs):
    bf16, f32 = jnp.bfloat16, jnp.float32
    anywhere = pl.BlockSpec(memory_space=pl.ANY)
    vmem = pl.BlockSpec(memory_space=pltpu.VMEM)
    return pl.pallas_call(
        kernel,
        out_shape=(
            jax.ShapeDtypeStruct((1024, LOCAL_COLS), bf16),
            jax.ShapeDtypeStruct((128, 1024), f32),
        ),
        in_specs=[anywhere, anywhere, anywhere, vmem],
        out_specs=(anywhere, anywhere),
        scratch_shapes=[
            pltpu.VMEM((2048, 1024), bf16),
            pltpu.VMEM((4, 1024, 512), bf16),
            pltpu.VMEM((4, 4, 2, 512, 128), bf16),
            pltpu.VMEM((4, 1024, 256), f32),
            pltpu.VMEM((3, 1024, 256), bf16),
            pltpu.VMEM((1024, 128), bf16),
            pltpu.VMEM((1024, 256), bf16),
            pltpu.VMEM((1024, 256), bf16),
            pltpu.VMEM((1024, 256), bf16),
            pltpu.VMEM((1024, 128), bf16),
            pltpu.VMEM((1024, LOCAL_COLS), bf16),
            pltpu.VMEM((64, LOCAL_COLS), f32),
            pltpu.VMEM((32, LOCAL_COLS), bf16),
            pltpu.VMEM((4, 2, 2, 32, LOCAL_COLS), bf16),
            pltpu.VMEM((4, 2, 2, 32, CORNER), bf16),
            pltpu.VMEM((1024, HALF), bf16),
            pltpu.VMEM((4, 2, 2, 128, HALF), bf16),
            pltpu.VMEM((1024, HALF), bf16),
            pltpu.VMEM((4, 128, 128), f32),
            pltpu.VMEM((2, 256, 256), f32),
            pltpu.VMEM((2, HALF, HALF), bf16),
            pltpu.VMEM((1, WIN), f32),
            pltpu.VMEM((4, 256, 128), bf16),
            pltpu.VMEM((2, 256, 1), jnp.int32),
            pltpu.VMEM((128, 1024), f32),
            pltpu.SemaphoreType.DMA((3,)),
            pltpu.SemaphoreType.DMA((2 * STEPS,)),
            pltpu.SemaphoreType.DMA((192,)),
            pltpu.SemaphoreType.DMA((112,)),
        ],
        compiler_params=pltpu.CompilerParams(
            collective_id=0, has_side_effects=True, vmem_limit_bytes=60 * 1024 * 1024
        ),
    )(features, weights, u_rows, keep_pairs.transpose(0, 2, 1))


def solution(mesh):
    in_specs = (P("dp", "mp"), P("mp", "dp"), P("mp", "dp"), P())
    out_specs = (P("mp", "dp"), P("dp", "mp"))
    return jax.shard_map(body, mesh=mesh, in_specs=in_specs, out_specs=out_specs, check_vma=False)
```

```python
import jax
import jax.numpy as jnp
from jax import lax
from jax.experimental import pallas as pl
from jax.experimental.pallas import tpu as pltpu
from jax.sharding import PartitionSpec as P

B = 512
PANELS = 2
WIN = 1024
TOKENS = 16384
HALF = WIN // 2
CORNER = HALF
LOCAL_COLS = 2048
STEPS = 16
LAG = 6
MESH = pl.DeviceIdType.MESH
EXACT = lax.Precision.HIGHEST


def iota(shape, dim):
    return lax.broadcasted_iota(jnp.int32, shape, dim)


def pruned_of(first, second):
    low = jnp.where(first != 0, 0, jnp.where(second != 1, 1, 2))
    high = jnp.where(second != 3, 3, jnp.where(first != 2, 2, 1))
    return low, high


def pruned_lanes(low, high):
    groups = low.shape[0]
    shape = (groups, 2 * groups)
    group, lane = iota(shape, 0), iota(shape, 1)
    own = jnp.where((lane & 1) == 0, low, high) + 4 * group
    return jnp.sum(jnp.where((lane >> 1) == group, own, 0), axis=0, keepdims=True)


def kept_lanes(low, high):
    groups = low.shape[0]
    shape = (groups, 4 * groups)
    group, lane = iota(shape, 0), iota(shape, 1)
    pruned = ((lane >> 2) == group) & (((lane & 3) == low) | ((lane & 3) == high))
    return 1.0 - jnp.sum(jnp.where(pruned, 1.0, 0.0), axis=0, keepdims=True)


def kernel(
    feat_hbm, w_hbm, u_hbm, pairs_ref, out_hbm, hess_hbm,
    feat, feat_t, win, acc, sums, to_pair, relay, from_left, from_right, from_pair,
    wv, uv, picked_rows, ug, cg, wcs, wcb, ev, parts, halves, inv, mask, picks, low_high, hout,
    local_sem, win_sem, send_sem, recv_sem,
):
    dp, mp = lax.axis_index("dp"), lax.axis_index("mp")
    x, l = lax.div(dp, 2), lax.rem(dp, 2)
    z, h, k = lax.div(mp, 4), lax.rem(lax.div(mp, 2), 2), lax.rem(mp, 2)
    is_source = mp == 0
    is_owner = dp == 0
    f32, bf16 = jnp.float32, jnp.bfloat16

    def at_mp(zz, hh, kk):
        return (dp, lax.rem(zz + 8, 4) * 4 + hh * 2 + kk)

    def at_dp(xx, ll):
        return (lax.rem(xx + 8, 4) * 2 + ll, mp)

    counter = [0]

    def take(n=1):
        counter[0] += n
        return counter[0] - n

    piece_landed = take(2 * STEPS)
    shared_landed = take(2 * STEPS)
    u_landed, c_landed, w_landed = take(5), take(5), take(5)
    picked_landed, corner_landed, part_landed = take(1), take(2), take(2)
    level_landed, inverse_landed, rows_landed = take(4), take(1), take(1)
    relay_landed, left_landed, right_landed, pair_landed = take(1), take(2), take(2), take(1)

    def remote(src, dst, sent, landed, device):
        return pltpu.make_async_remote_copy(
            src_ref=src, dst_ref=dst, send_sem=send_sem.at[sent], recv_sem=recv_sem.at[landed],
            device_id=device, device_id_type=MESH,
        )

    def arrived(dst, landed):
        remote(dst, dst, 0, landed, at_mp(z, h, 1 - k)).wait_recv()

    load_u = pltpu.make_async_copy(u_hbm, uv, local_sem.at[0])
    load_f = pltpu.make_async_copy(feat_hbm, feat, local_sem.at[1])
    load_w = pltpu.make_async_copy(w_hbm, wv, local_sem.at[2])
    load_u.start()

    def window_block(i, half):
        t, tq = divmod(i, 4)
        if t == 0 or t == 3:
            owner = lax.rem(x + (2 if t == 0 else 0), 4) * 2 + (l if half else 1 - l)
        else:
            owner = lax.rem(x + (3 if half else 1), 4) * 2 + (1 - l if t == 1 else l)
        column = pl.multiple_of(owner * 128, 128)
        return pltpu.make_async_copy(
            feat_hbm.at[pl.ds(tq * 512, 512), pl.ds(column, 128)], win.at[t, tq, half], win_sem.at[2 * i + half]
        )

    @pl.when(is_source)
    def _():
        for i in range(STEPS):
            for half in range(2):
                window_block(i, half).start()

    load_w.start()
    load_f.start()

    barrier = pltpu.get_barrier_semaphore()
    peers = [(lax.rem(dp + o, 8), mp) for o in range(1, 8)]
    peers += [(lax.rem(dp + o, 8), mp + 1 - 2 * k) for o in range(1, 8)]
    peers += [at_mp(z + 1, h, k), at_mp(z - 1, h, k), at_mp(z, 1 - h, k), at_mp(z, h, 1 - k)]
    for peer in peers:
        pl.semaphore_signal(barrier, inc=1, device_id=peer, device_id_type=MESH)

    wide = jnp.concatenate([pairs_ref[0], pairs_ref[1], pairs_ref[0], pairs_ref[1]], axis=0).astype(f32)
    tall = wide.T.astype(jnp.int32)
    for panel in range(PANELS):
        low, high = pruned_of(tall[:, 2 * panel : 2 * panel + 1], tall[:, 2 * panel + 1 : 2 * panel + 2])
        low_high[0, panel * 128 : (panel + 1) * 128, :] = low
        low_high[1, panel * 128 : (panel + 1) * 128, :] = high
    for c in range(4):
        low, high = low_high[0, c * 64 : (c + 1) * 64, :], low_high[1, c * 64 : (c + 1) * 64, :]
        picks[c] = (iota((256, 128), 0) == pruned_lanes(low, high)).astype(bf16)
        mask[:, c * 256 : (c + 1) * 256] = jnp.where(is_owner, kept_lanes(low, high), 1.0)

    own_groups = pl.ds(pl.multiple_of(mp * 16, 16), 16)
    own_rows = pruned_lanes(low_high[0, own_groups, :], low_high[1, own_groups, :])
    row_pick = (iota((64, 32), 0) == own_rows).astype(bf16)
    load_u.wait()
    picked = lax.dot_general(
        row_pick, uv[...].astype(bf16), (((0,), (0,)), ((), ())), preferred_element_type=f32
    ).astype(bf16)
    picked_rows[...] = picked

    @pl.when(k == 1)
    def _():
        ug[z, h, 1] = picked


    @pl.when(is_owner)
    def _():
        for c in range(4):
            cg[z, h, k, :, c * 128 : (c + 1) * 128] = jnp.dot(
                picked[:, c * 256 : (c + 1) * 256], picks[c], preferred_element_type=f32
            ).astype(bf16)

    pl.semaphore_wait(barrier, len(peers))

    def pick_weights():
        load_w.wait()

        @pl.when(is_owner)
        def _():
            for c in range(4):
                wcs[:, c * 128 : (c + 1) * 128] = jnp.dot(
                    wv[:, c * 256 : (c + 1) * 256], picks[c], preferred_element_type=f32
                ).astype(bf16)

    def transpose_features():
        load_f.wait()

        @pl.loop(0, 8)
        def _(tb):
            block = feat[pl.ds(pl.multiple_of(tb * 256, 256), 256), :]
            feat_t[lax.div(tb, 2), :, pl.ds(pl.multiple_of(lax.rem(tb, 2) * 256, 256), 256)] = block.T

    def product(i):
        t, tq = divmod(i, 4)

        @pl.loop(0, 2)
        def _(m):
            rows = pl.ds(pl.multiple_of(m * 512, 512), 512)
            columns = jnp.concatenate([win[t, tq, 0], win[t, tq, 1]], axis=1)
            part = jnp.dot(feat_t[tq, rows, :], columns, preferred_element_type=f32)
            if tq == 0:
                acc[t, rows, :] = part
            else:
                acc[t, rows, :] += part

    def add_to(slot, half, source):
        cols = pl.ds(half * 128, 128)

        @pl.loop(0, 4)
        def _(m):
            rows = pl.ds(pl.multiple_of(m * 256, 256), 256)
            acc[slot, rows, cols] += source[rows, :].astype(f32)

    def round_sum(slot, half):
        cols = pl.ds(half * 128, 128)

        @pl.loop(0, 4)
        def _(m):
            rows = pl.ds(pl.multiple_of(m * 256, 256), 256)
            sums[slot, half, rows, :] = acc[slot, rows, cols].astype(bf16)

    def update_columns(c):
        cols = pl.ds(c * 256, 256)
        factor = ug[:, :, :, :, cols].reshape(HALF, 256)
        updated = wv[:, cols].astype(f32) - jnp.dot(ev[...], factor, preferred_element_type=f32)
        if c < 4:
            updated = updated * mask[:, c * 256 : (c + 1) * 256]
        wv[:, cols] = updated.astype(bf16)

    def solve_rows(core):
        @pl.loop(0, 2)
        def _(m):
            lead = wcb[pl.ds(m * 2, 2), :, core].reshape(512, HALF)
            rows = pl.ds(pl.multiple_of(m * 512, 512), 512)
            first = lead[:, 0:256]
            ev[rows, 0:256] = (
                jnp.dot(first, inv[0, 0:256, 0:256], preferred_element_type=f32)
                + jnp.dot(first, inv[1, 0:256, 0:256], preferred_element_type=f32)
            ).astype(bf16)
            ev[rows, 256:] = (
                jnp.dot(lead, inv[0, :, 256:], preferred_element_type=f32)
                + jnp.dot(lead, inv[1, :, 256:], preferred_element_type=f32)
            ).astype(bf16)

    store_w = pltpu.make_async_copy(wv, out_hbm, local_sem.at[0])
    store_h = pltpu.make_async_copy(hout, hess_hbm, local_sem.at[1])

    def run(core):
        way = 1 - 2 * core
        pending = []
        sends = [0]
        partner = at_mp(z, h, 1 - core)

        def send(src, dst, landed, device, when=None):
            sent = sends[0]
            sends[0] += 1
            make = lambda: remote(src, dst, sent, landed, device)
            if when is None:
                make().start()
            else:
                pl.when(when)(lambda: make().start())
            pending.append((when, make))

        def send_sum(slot, half):
            round_sum(slot, half)
            if half == 0:
                send(sums.at[slot, 0], from_left.at[slot - 1], left_landed + slot - 1, at_dp(x + 1, l))
            else:
                send(sums.at[slot, 1], from_right.at[slot - 1], right_landed + slot - 1, at_dp(x - 1, l))

        def reduce_pairs(i):
            if i == 3:
                round_sum(0, 0)
                round_sum(0, 1)
                send(sums.at[0], relay, relay_landed, at_dp(x + way, l))
            if i == 7:
                send_sum(1, 1 - core)
            if i == 9:
                arrived(relay, relay_landed)
                add_to(1, core, relay.at[0])
                send_sum(1, core)
            if i == 11:
                send_sum(2, 1 - core)
                add_to(2, core, relay.at[1])
                send_sum(2, core)

        def own_sum(n):
            arrived(from_left.at[n], left_landed + n)
            arrived(from_right.at[n], right_landed + n)
            total = acc[3, :, n * 128 : (n + 1) * 128] + from_left[n].astype(f32)
            return total + from_right[n].astype(f32)

        def send_pair():
            to_pair[...] = own_sum(0).astype(bf16)
            send(to_pair, from_pair, pair_landed, at_dp(x, 1 - l))

        def finish_hessian():
            total = own_sum(1)
            arrived(from_pair, pair_landed)
            hout[...] = ((total + from_pair[...].astype(f32)) * (2.0 / TOKENS)).T
            store_h.start()

        def send_corner():
            for o in range(7, -1, -1):
                device = (jnp.int32(o), mp + 1 - core)
                if o == 0:
                    if core == 0:
                        send(cg.at[z, h, 0], cg.at[z, h, 0], corner_landed, device, when=is_owner)
                else:
                    send(cg.at[z, h, core], cg.at[z, h, core], corner_landed + core, device, when=is_owner)

        def send_weights():
            pick_weights()
            for o in range(7, -1, -1):
                device = (jnp.int32(o), mp + 1 - core)
                part = wcs.at[pl.ds(o * 128, 128), :]
                target = wcb.at[o // 2, o % 2, core]
                if o == 0:
                    if core == 0:
                        send(part, target, part_landed, device, when=is_owner)
                else:
                    send(part, target, part_landed + core, device, when=is_owner)

        if core == 0:
            late = jnp.where((z == 1) | (z == 3), LAG, 0)
            early_set = jnp.where(z == 3, 1, 0)
            send_base = 0

            def piece(i, half):
                return win.at[lax.div(i, 4), lax.rem(i, 4), half]

            def routes(half):
                step = 1 - 2 * half
                r = lax.rem(z * step + 4, 4)
                on_first = h == 0
                forward = (on_first & (r < 3)) | ((h == 1) & ((r == 1) | (r == 2)))
                cross = on_first & (r == 1)
                back = (h == 1) & (r == 1)
                return (
                    (forward, at_mp(z + step, h, 0), 0),
                    (cross, at_mp(z, 1, 0), 1),
                    (back, at_mp(z - step, h, 0), 2),
                )

            def copies(i, half):
                ref = piece(i, half)
                slot = 2 * i + half
                for when, device, kind in routes(half):
                    yield when, remote(ref, ref, 4 * slot + kind, piece_landed + slot, device)
                yield None, remote(ref, ref, 4 * slot + 3, shared_landed + slot, partner)

            def pass_on(i, half):
                for when, copy in copies(i, half):
                    if when is None:
                        copy.start()
                    else:
                        pl.when(when)(copy.start)

            sends[0] = 8 * STEPS

            def start_pieces(some):
                @pl.when(is_source)
                def _():
                    for i in some:
                        for half in range(2):
                            window_block(i, half).wait()
                            pass_on(i, half)

            send_corner()
            send(picked_rows, ug.at[z, h, 0], picked_landed, partner)
            start_pieces(range(4))
            send_weights()
            start_pieces(range(4, STEPS))
            transpose_features()

            def take_piece(i, half):
                arrived(piece(i, half), piece_landed + 2 * i + half)
                pass_on(i, half)

            for step in range(STEPS + LAG):
                if step < STEPS:
                    pl.when(jnp.logical_not(is_source))(lambda: take_piece(step, early_set))
                index = step - late
                ready = jnp.logical_not(is_source) & (index >= 0) & (index < STEPS)
                pl.when(ready)(lambda: take_piece(index, 1 - early_set))
                i = step - LAG
                if i >= 0:
                    product(i)
                    reduce_pairs(i)

            send_pair()
            arrived(inv, inverse_landed)
            arrived(wcb.at[:, :, 0], rows_landed)
            solve_rows(0)
            for n, zz in enumerate((z, z + 3, z + 1, z + 2)):
                arrived(ug.at[lax.rem(zz, 4)], level_landed + n)
            for c in range(8):
                update_columns(c)
            store_w.start()
            finish_hessian()
            for i in range(STEPS):
                for half in range(2):
                    for when, copy in copies(jnp.int32(i), half):
                        if when is None:
                            copy.wait_send()
                        else:
                            pl.when(when)(copy.wait_send)
        else:

            class Gather:
                def __init__(self, buffer, landed, pos, line, device):
                    self.buffer, self.pos, self.line, self.device = buffer, pos, line, device
                    self.landed = landed
                    self.after = lax.rem(pos + 1, 4)
                    self.before = lax.rem(pos + 3, 4)
                    self.far = lax.rem(pos + 2, 4)

                def move(self, view, n, device):
                    send(view, view, self.landed + n, device)

                def first(self):
                    self.move(self.buffer.at[self.pos, self.line], 0, self.device(self.pos, 1 - self.line))

                def second(self):
                    arrived(self.buffer.at[self.pos, 1 - self.line], self.landed)
                    own = self.buffer.at[self.pos]
                    self.move(own, 1, self.device(self.pos + 1, self.line))
                    self.move(own, 2, self.device(self.pos - 1, self.line))

                def third(self):
                    arrived(self.buffer.at[self.before], self.landed + 1)
                    arrived(self.buffer.at[self.after], self.landed + 2)
                    self.move(self.buffer.at[self.before, 0], 3, self.device(self.pos + 1, self.line))
                    self.move(self.buffer.at[self.after, 1], 4, self.device(self.pos - 1, self.line))

                def finish(self):
                    arrived(self.buffer.at[self.far, 0], self.landed + 3)
                    arrived(self.buffer.at[self.far, 1], self.landed + 4)

            over_mp = lambda p, q: at_mp(p, q, 1)
            u_gather = Gather(ug, u_landed, z, h, over_mp)
            c_gather = Gather(cg, c_landed, z, h, over_mp)
            w_gather = Gather(wcb, w_landed, x, l, at_dp)
            levels = (u_gather.pos, u_gather.before, u_gather.after, u_gather.far)

            def share_level(n):
                send(ug.at[levels[n]], ug.at[levels[n]], level_landed + n, partner)

            row, col = iota((128, 128), 0), iota((128, 128), 1)

            def system(i, j, rows, cols):
                view = cg[i : i + rows // 128, :, :, :, j * 128 : j * 128 + cols]
                return view.reshape(rows, cols).astype(f32)

            def exact_dot(a, b):
                return jnp.dot(a, b, precision=EXACT)

            def invert_diagonal():
                for j in range(4):
                    block = system(j, j, 128, 128)
                    parts[j] = jnp.where(row == col, 1.0 / jnp.where(row == col, block, 1.0), 0.0)

            def invert_level(level):
                same = (row >> (level + 1)) == (col >> (level + 1))
                upper_part = ((row >> level) + 1 == (col >> level)) & same
                steps = [exact_dot(jnp.where(upper_part, system(j, j, 128, 128), 0.0), parts[j]) for j in range(4)]
                for j in range(4):
                    parts[j] = parts[j] - exact_dot(parts[j], steps[j])

            def invert_halves():
                for j in range(2):
                    low, high = parts[2 * j], parts[2 * j + 1]
                    halves[j, 0:128, 0:128] = low
                    halves[j, 128:, 128:] = high
                    halves[j, 128:, 0:128] = jnp.zeros((128, 128), f32)
                    halves[j, 0:128, 128:] = -exact_dot(low, exact_dot(system(2 * j, 2 * j + 1, 128, 128), high))

            def keep_split(part, rows, cols):
                rounded = part.astype(bf16)
                inv[0, rows : rows + 256, cols : cols + 256] = rounded
                inv[1, rows : rows + 256, cols : cols + 256] = (part - rounded.astype(f32)).astype(bf16)

            def invert_whole():
                keep_split(halves[0], 0, 0)
                keep_split(halves[1], 256, 256)
                keep_split(-exact_dot(halves[0], exact_dot(system(0, 2, 256, 256), halves[1])), 0, 256)
                for n in range(2):
                    inv[n, 256:, 0:256] = jnp.zeros((256, 256), bf16)
                send(inv, inv, inverse_landed, partner)

            def consume(i):
                for half in range(2):
                    arrived(win.at[i // 4, i % 4, half], shared_landed + 2 * i + half)
                product(i)
                reduce_pairs(i)

            def start_u():
                arrived(ug.at[z, h, 0], picked_landed)
                u_gather.first()

            def start_c():
                arrived(cg.at[z, h, 0], corner_landed)
                pl.when(jnp.logical_not(is_owner))(lambda: arrived(cg.at[z, h, 1], corner_landed + 1))
                c_gather.first()

            def start_w():
                @pl.when(is_owner)
                def _():
                    wcb[0, 0, 1] = wcs[0:128, :]

                arrived(wcb.at[x, l, 0], part_landed)
                pl.when(jnp.logical_not(is_owner))(lambda: arrived(wcb.at[x, l, 1], part_landed + 1))
                w_gather.first()

            def third_u():
                u_gather.third()
                for n in range(3):
                    share_level(n)

            def finish_u():
                u_gather.finish()
                share_level(3)

            def finish_w():
                w_gather.finish()
                send(wcb.at[:, :, 0], wcb.at[:, :, 0], rows_landed, partner)

            send_corner()
            start_u()
            send_weights()
            start_c()
            transpose_features()
            c_gather.second()
            c_gather.third()
            u_gather.second()
            start_w()
            c_gather.finish()
            consume(0)
            invert_diagonal()
            invert_level(0)
            invert_level(1)
            w_gather.second()
            consume(1)
            invert_level(2)
            invert_level(3)
            consume(2)
            third_u()
            consume(3)
            for n in range(4, 7):
                invert_level(n)
            w_gather.third()
            consume(4)
            invert_halves()
            consume(5)
            invert_whole()
            finish_u()
            consume(6)
            consume(7)
            finish_w()
            consume(8)
            consume(9)
            solve_rows(1)
            for i in range(10, STEPS):
                update_columns(i - 10)
                consume(i)
            send_pair()
            update_columns(6)
            update_columns(7)
            store_w.start()
            finish_hessian()

        for when, make in pending:
            if when is None:
                make().wait_send()
            else:
                pl.when(when)(lambda: make().wait_send())
        store_w.wait()
        store_h.wait()

    pl.when(k == 0)(lambda: run(0))
    pl.when(k == 1)(lambda: run(1))


def body(features, weights, u_rows, keep_pairs):
    bf16, f32 = jnp.bfloat16, jnp.float32
    anywhere = pl.BlockSpec(memory_space=pl.ANY)
    vmem = pl.BlockSpec(memory_space=pltpu.VMEM)
    return pl.pallas_call(
        kernel,
        out_shape=(
            jax.ShapeDtypeStruct((1024, LOCAL_COLS), bf16),
            jax.ShapeDtypeStruct((128, 1024), f32),
        ),
        in_specs=[anywhere, anywhere, anywhere, vmem],
        out_specs=(anywhere, anywhere),
        scratch_shapes=[
            pltpu.VMEM((2048, 1024), bf16),
            pltpu.VMEM((4, 1024, 512), bf16),
            pltpu.VMEM((4, 4, 2, 512, 128), bf16),
            pltpu.VMEM((4, 1024, 256), f32),
            pltpu.VMEM((3, 2, 1024, 128), bf16),
            pltpu.VMEM((1024, 128), bf16),
            pltpu.VMEM((2, 1024, 128), bf16),
            pltpu.VMEM((2, 1024, 128), bf16),
            pltpu.VMEM((2, 1024, 128), bf16),
            pltpu.VMEM((1024, 128), bf16),
            pltpu.VMEM((1024, LOCAL_COLS), bf16),
            pltpu.VMEM((64, LOCAL_COLS), f32),
            pltpu.VMEM((32, LOCAL_COLS), bf16),
            pltpu.VMEM((4, 2, 2, 32, LOCAL_COLS), bf16),
            pltpu.VMEM((4, 2, 2, 32, CORNER), bf16),
            pltpu.VMEM((1024, HALF), bf16),
            pltpu.VMEM((4, 2, 2, 128, HALF), bf16),
            pltpu.VMEM((1024, HALF), bf16),
            pltpu.VMEM((4, 128, 128), f32),
            pltpu.VMEM((2, 256, 256), f32),
            pltpu.VMEM((2, HALF, HALF), bf16),
            pltpu.VMEM((1, WIN), f32),
            pltpu.VMEM((4, 256, 128), bf16),
            pltpu.VMEM((2, 256, 1), jnp.int32),
            pltpu.VMEM((128, 1024), f32),
            pltpu.SemaphoreType.DMA((3,)),
            pltpu.SemaphoreType.DMA((2 * STEPS,)),
            pltpu.SemaphoreType.DMA((192,)),
            pltpu.SemaphoreType.DMA((112,)),
        ],
        compiler_params=pltpu.CompilerParams(
            collective_id=0, has_side_effects=True, vmem_limit_bytes=47 * 1024 * 1024
        ),
    )(features, weights, u_rows, keep_pairs.transpose(0, 2, 1))


def solution(mesh):
    in_specs = (P("dp", "mp"), P("mp", "dp"), P("mp", "dp"), P())
    out_specs = (P("mp", "dp"), P("dp", "mp"))
    return jax.shard_map(body, mesh=mesh, in_specs=in_specs, out_specs=out_specs, check_vma=False)
```

```python
import jax
import jax.numpy as jnp
from jax import lax
from jax.experimental import pallas as pl
from jax.experimental.pallas import tpu as pltpu
from jax.sharding import PartitionSpec as P

B = 512
PANELS = 2
WIN = 1024
TOKENS = 16384
HALF = WIN // 2
CORNER = HALF
LOCAL_COLS = 2048
STEPS = 16
LAG = 6
MESH = pl.DeviceIdType.MESH
EXACT = lax.Precision.HIGHEST


def iota(shape, dim):
    return lax.broadcasted_iota(jnp.int32, shape, dim)


def pruned_of(first, second):
    low = jnp.where(first != 0, 0, jnp.where(second != 1, 1, 2))
    high = jnp.where(second != 3, 3, jnp.where(first != 2, 2, 1))
    return low, high


def pruned_lanes(low, high):
    groups = low.shape[0]
    shape = (groups, 2 * groups)
    group, lane = iota(shape, 0), iota(shape, 1)
    own = jnp.where((lane & 1) == 0, low, high) + 4 * group
    return jnp.sum(jnp.where((lane >> 1) == group, own, 0), axis=0, keepdims=True)


def kept_lanes(low, high):
    groups = low.shape[0]
    shape = (groups, 4 * groups)
    group, lane = iota(shape, 0), iota(shape, 1)
    pruned = ((lane >> 2) == group) & (((lane & 3) == low) | ((lane & 3) == high))
    return 1.0 - jnp.sum(jnp.where(pruned, 1.0, 0.0), axis=0, keepdims=True)


def kernel(
    feat_hbm, w_hbm, u_hbm, pairs_ref, out_hbm, hess_hbm,
    feat, feat_t, win, acc, sums, to_pair, relay, from_left, from_right, from_pair,
    wv, uv, picked_rows, ug, cg, wcs, wcb, ev, parts, halves, inv, mask, picks, low_high, hout,
    local_sem, win_sem, send_sem, recv_sem,
):
    dp, mp = lax.axis_index("dp"), lax.axis_index("mp")
    x, l = lax.div(dp, 2), lax.rem(dp, 2)
    z, h, k = lax.div(mp, 4), lax.rem(lax.div(mp, 2), 2), lax.rem(mp, 2)
    is_source = mp == 0
    is_owner = dp == 0
    f32, bf16 = jnp.float32, jnp.bfloat16

    def at_mp(zz, hh, kk):
        return (dp, lax.rem(zz + 8, 4) * 4 + hh * 2 + kk)

    def at_dp(xx, ll):
        return (lax.rem(xx + 8, 4) * 2 + ll, mp)

    counter = [0]

    def take(n=1):
        counter[0] += n
        return counter[0] - n

    piece_landed = take(2 * STEPS)
    shared_landed = take(2 * STEPS)
    u_landed, c_landed, w_landed = take(5), take(5), take(5)
    picked_landed, corner_landed, part_landed = take(1), take(2), take(2)
    level_landed, inverse_landed, rows_landed = take(4), take(1), take(1)
    relay_landed, left_landed, right_landed, pair_landed = take(1), take(2), take(2), take(1)

    def remote(src, dst, sent, landed, device):
        return pltpu.make_async_remote_copy(
            src_ref=src, dst_ref=dst, send_sem=send_sem.at[sent], recv_sem=recv_sem.at[landed],
            device_id=device, device_id_type=MESH,
        )

    def arrived(dst, landed):
        remote(dst, dst, 0, landed, at_mp(z, h, 1 - k)).wait_recv()

    load_u = pltpu.make_async_copy(u_hbm, uv, local_sem.at[0])
    load_f = pltpu.make_async_copy(feat_hbm, feat, local_sem.at[1])
    load_w = pltpu.make_async_copy(w_hbm, wv, local_sem.at[2])
    load_u.start()

    def window_block(i, half):
        t, tq = divmod(i, 4)
        if t == 0 or t == 3:
            owner = lax.rem(x + (2 if t == 0 else 0), 4) * 2 + (l if half else 1 - l)
        else:
            owner = lax.rem(x + (3 if half else 1), 4) * 2 + (1 - l if t == 1 else l)
        column = pl.multiple_of(owner * 128, 128)
        return pltpu.make_async_copy(
            feat_hbm.at[pl.ds(tq * 512, 512), pl.ds(column, 128)], win.at[t, tq, half], win_sem.at[2 * i + half]
        )

    @pl.when(is_source)
    def _():
        for i in range(STEPS):
            for half in range(2):
                window_block(i, half).start()

    load_w.start()
    load_f.start()

    barrier = pltpu.get_barrier_semaphore()
    peers = [(lax.rem(dp + o, 8), mp) for o in range(1, 8)]
    peers += [(lax.rem(dp + o, 8), mp + 1 - 2 * k) for o in range(1, 8)]
    peers += [at_mp(z + 1, h, k), at_mp(z - 1, h, k), at_mp(z, 1 - h, k), at_mp(z, h, 1 - k)]
    for peer in peers:
        pl.semaphore_signal(barrier, inc=1, device_id=peer, device_id_type=MESH)

    wide = jnp.concatenate([pairs_ref[0], pairs_ref[1], pairs_ref[0], pairs_ref[1]], axis=0).astype(f32)
    tall = wide.T.astype(jnp.int32)
    for panel in range(PANELS):
        low, high = pruned_of(tall[:, 2 * panel : 2 * panel + 1], tall[:, 2 * panel + 1 : 2 * panel + 2])
        low_high[0, panel * 128 : (panel + 1) * 128, :] = low
        low_high[1, panel * 128 : (panel + 1) * 128, :] = high
    for c in range(4):
        low, high = low_high[0, c * 64 : (c + 1) * 64, :], low_high[1, c * 64 : (c + 1) * 64, :]
        picks[c] = (iota((256, 128), 0) == pruned_lanes(low, high)).astype(bf16)
        mask[:, c * 256 : (c + 1) * 256] = jnp.where(is_owner, kept_lanes(low, high), 1.0)

    own_groups = pl.ds(pl.multiple_of(mp * 16, 16), 16)
    own_rows = pruned_lanes(low_high[0, own_groups, :], low_high[1, own_groups, :])
    row_pick = (iota((64, 32), 0) == own_rows).astype(bf16)
    load_u.wait()
    picked = lax.dot_general(
        row_pick, uv[...].astype(bf16), (((0,), (0,)), ((), ())), preferred_element_type=f32
    ).astype(bf16)
    picked_rows[...] = picked

    @pl.when(k == 1)
    def _():
        ug[z, h, 1] = picked


    @pl.when(is_owner)
    def _():
        for c in range(4):
            cg[z, h, k, :, c * 128 : (c + 1) * 128] = jnp.dot(
                picked[:, c * 256 : (c + 1) * 256], picks[c], preferred_element_type=f32
            ).astype(bf16)

    pl.semaphore_wait(barrier, len(peers))

    def pick_weights():
        load_w.wait()

        @pl.when(is_owner)
        def _():
            for c in range(4):
                wcs[:, c * 128 : (c + 1) * 128] = jnp.dot(
                    wv[:, c * 256 : (c + 1) * 256], picks[c], preferred_element_type=f32
                ).astype(bf16)

    def transpose_features():
        load_f.wait()

        @pl.loop(0, 8)
        def _(tb):
            block = feat[pl.ds(pl.multiple_of(tb * 256, 256), 256), :]
            feat_t[lax.div(tb, 2), :, pl.ds(pl.multiple_of(lax.rem(tb, 2) * 256, 256), 256)] = block.T

    def product(i):
        t, tq = divmod(i, 4)

        @pl.loop(0, 2)
        def _(m):
            rows = pl.ds(pl.multiple_of(m * 512, 512), 512)
            columns = jnp.concatenate([win[t, tq, 0], win[t, tq, 1]], axis=1)
            part = jnp.dot(feat_t[tq, rows, :], columns, preferred_element_type=f32)
            if tq == 0:
                acc[t, rows, :] = part
            else:
                acc[t, rows, :] += part

    def add_to(slot, half, source):
        cols = pl.ds(half * 128, 128)

        @pl.loop(0, 4)
        def _(m):
            rows = pl.ds(pl.multiple_of(m * 256, 256), 256)
            acc[slot, rows, cols] += source[rows, :].astype(f32)

    def round_sum(slot, half):
        cols = pl.ds(half * 128, 128)

        @pl.loop(0, 4)
        def _(m):
            rows = pl.ds(pl.multiple_of(m * 256, 256), 256)
            sums[slot, half, rows, :] = acc[slot, rows, cols].astype(bf16)

    def update_columns(c):
        cols = pl.ds(c * 256, 256)
        factor = ug[:, :, :, :, cols].reshape(HALF, 256)
        updated = wv[:, cols].astype(f32) - jnp.dot(ev[...], factor, preferred_element_type=f32)
        if c < 4:
            updated = updated * mask[:, c * 256 : (c + 1) * 256]
        wv[:, cols] = updated.astype(bf16)

    def solve_rows(core):
        @pl.loop(0, 2)
        def _(m):
            lead = wcb[pl.ds(m * 2, 2), :, core].reshape(512, HALF)
            rows = pl.ds(pl.multiple_of(m * 512, 512), 512)
            first = lead[:, 0:256]
            ev[rows, 0:256] = (
                jnp.dot(first, inv[0, 0:256, 0:256], preferred_element_type=f32)
                + jnp.dot(first, inv[1, 0:256, 0:256], preferred_element_type=f32)
            ).astype(bf16)
            ev[rows, 256:] = (
                jnp.dot(lead, inv[0, :, 256:], preferred_element_type=f32)
                + jnp.dot(lead, inv[1, :, 256:], preferred_element_type=f32)
            ).astype(bf16)

    store_w = pltpu.make_async_copy(wv, out_hbm, local_sem.at[0])
    store_h = pltpu.make_async_copy(hout, hess_hbm, local_sem.at[1])

    def run(core):
        way = 1 - 2 * core
        pending = []
        sends = [0]
        partner = at_mp(z, h, 1 - core)
        right, left, onward = at_dp(x + 1, l), at_dp(x - 1, l), at_dp(x + way, l)

        def send(src, dst, landed, device, when=None):
            sent = sends[0]
            sends[0] += 1
            made = lambda ref: ref() if callable(ref) else ref
            make = lambda: remote(made(src), made(dst), sent, landed, device)
            if when is None:
                make().start()
            else:
                pl.when(when)(lambda: make().start())
            pending.append((when, make))

        def send_sum(slot, half):
            round_sum(slot, half)
            if half == 0:
                send(lambda: sums.at[slot, 0], lambda: from_left.at[slot - 1], left_landed + slot - 1, right)
            else:
                send(lambda: sums.at[slot, 1], lambda: from_right.at[slot - 1], right_landed + slot - 1, left)

        def reduce_pairs(i):
            if i == 3:
                round_sum(0, 0)
                round_sum(0, 1)
                send(lambda: sums.at[0], relay, relay_landed, onward)
            if i == 7:
                send_sum(1, 1 - core)
            if i == 9:
                arrived(relay, relay_landed)
                add_to(1, core, relay.at[0])
                send_sum(1, core)
            if i == 11:
                send_sum(2, 1 - core)
                add_to(2, core, relay.at[1])
                send_sum(2, core)

        def own_sum(n):
            arrived(from_left.at[n], left_landed + n)
            arrived(from_right.at[n], right_landed + n)
            total = acc[3, :, n * 128 : (n + 1) * 128] + from_left[n].astype(f32)
            return total + from_right[n].astype(f32)

        def send_pair():
            to_pair[...] = own_sum(0).astype(bf16)
            send(to_pair, from_pair, pair_landed, at_dp(x, 1 - l))

        def finish_hessian():
            total = own_sum(1)
            arrived(from_pair, pair_landed)
            hout[...] = ((total + from_pair[...].astype(f32)) * (2.0 / TOKENS)).T
            store_h.start()

        def send_corner():
            for o in range(7, -1, -1):
                device = (jnp.int32(o), mp + 1 - core)
                if o == 0:
                    if core == 0:
                        send(cg.at[z, h, 0], cg.at[z, h, 0], corner_landed, device, when=is_owner)
                else:
                    send(cg.at[z, h, core], cg.at[z, h, core], corner_landed + core, device, when=is_owner)

        def send_weights():
            pick_weights()
            for o in range(7, -1, -1):
                device = (jnp.int32(o), mp + 1 - core)
                part = wcs.at[pl.ds(o * 128, 128), :]
                target = wcb.at[o // 2, o % 2, core]
                if o == 0:
                    if core == 0:
                        send(part, target, part_landed, device, when=is_owner)
                else:
                    send(part, target, part_landed + core, device, when=is_owner)

        if core == 0:
            uneven = (z == 1) | (z == 3)
            follower = jnp.logical_not(is_source)
            early_set = jnp.where(z == 3, 1, 0)

            def piece(i, half):
                return win.at[i // 4, i % 4, half]

            def routes(half):
                step = 1 - 2 * half
                r = lax.rem(z * step + 4, 4)
                on_first = h == 0
                forward = (on_first & (r < 3)) | ((h == 1) & ((r == 1) | (r == 2)))
                cross = on_first & (r == 1)
                back = (h == 1) & (r == 1)
                return (
                    (forward, at_mp(z + step, h, 0), 0),
                    (cross, at_mp(z, 1, 0), 1),
                    (back, at_mp(z - step, h, 0), 2),
                )

            def copies(i, half):
                ref = piece(i, half)
                slot = 2 * i + half
                for when, device, kind in routes(half):
                    yield when, remote(ref, ref, 4 * slot + kind, piece_landed + slot, device)
                yield None, remote(ref, ref, 4 * slot + 3, shared_landed + slot, partner)

            def pass_on(i, half):
                for when, copy in copies(i, half):
                    if when is None:
                        copy.start()
                    else:
                        pl.when(when)(copy.start)

            sends[0] = 8 * STEPS

            def start_pieces(some):
                @pl.when(is_source)
                def _():
                    for i in some:
                        for half in range(2):
                            window_block(i, half).wait()
                            pass_on(i, half)

            send_corner()
            send(picked_rows, ug.at[z, h, 0], picked_landed, partner)
            start_pieces(range(4))
            send_weights()
            start_pieces(range(4, STEPS))
            transpose_features()

            def take_piece(i, half):
                arrived(piece(i, half), piece_landed + 2 * i + half)
                pass_on(i, half)

            def relay_all(trail, lag):
                for step in range(STEPS + lag):
                    if step < STEPS:
                        pl.when(follower)(lambda: take_piece(step, early_set))
                    if 0 <= step - trail < STEPS:
                        pl.when(follower)(lambda: take_piece(step - trail, 1 - early_set))
                    i = step - lag
                    if i >= 0:
                        product(i)
                        reduce_pairs(i)

            mark = (sends[0], len(pending))
            pl.when(uneven)(lambda: relay_all(LAG, LAG))
            sends[0] = mark[0]
            del pending[mark[1] :]
            pl.when(jnp.logical_not(uneven))(lambda: relay_all(0, 1))
            send_pair()
            arrived(inv, inverse_landed)
            arrived(wcb.at[:, :, 0], rows_landed)
            solve_rows(0)
            for n, zz in enumerate((z, z + 3, z + 1, z + 2)):
                arrived(ug.at[lax.rem(zz, 4)], level_landed + n)
            for c in range(8):
                update_columns(c)
            store_w.start()
            finish_hessian()
            for i in range(STEPS):
                for half in range(2):
                    for when, copy in copies(i, half):
                        if when is None:
                            copy.wait_send()
                        else:
                            pl.when(when)(copy.wait_send)
        else:

            class Gather:
                def __init__(self, buffer, landed, pos, line, device):
                    self.buffer, self.pos, self.line, self.device = buffer, pos, line, device
                    self.landed = landed
                    self.after = lax.rem(pos + 1, 4)
                    self.before = lax.rem(pos + 3, 4)
                    self.far = lax.rem(pos + 2, 4)

                def move(self, view, n, device):
                    send(view, view, self.landed + n, device)

                def first(self):
                    self.move(self.buffer.at[self.pos, self.line], 0, self.device(self.pos, 1 - self.line))

                def second(self):
                    arrived(self.buffer.at[self.pos, 1 - self.line], self.landed)
                    own = self.buffer.at[self.pos]
                    self.move(own, 1, self.device(self.pos + 1, self.line))
                    self.move(own, 2, self.device(self.pos - 1, self.line))

                def third(self):
                    arrived(self.buffer.at[self.before], self.landed + 1)
                    arrived(self.buffer.at[self.after], self.landed + 2)
                    self.move(self.buffer.at[self.before, 0], 3, self.device(self.pos + 1, self.line))
                    self.move(self.buffer.at[self.after, 1], 4, self.device(self.pos - 1, self.line))

                def finish(self):
                    arrived(self.buffer.at[self.far, 0], self.landed + 3)
                    arrived(self.buffer.at[self.far, 1], self.landed + 4)

            over_mp = lambda p, q: at_mp(p, q, 1)
            u_gather = Gather(ug, u_landed, z, h, over_mp)
            c_gather = Gather(cg, c_landed, z, h, over_mp)
            w_gather = Gather(wcb, w_landed, x, l, at_dp)
            levels = (u_gather.pos, u_gather.before, u_gather.after, u_gather.far)

            def share_level(n):
                send(ug.at[levels[n]], ug.at[levels[n]], level_landed + n, partner)

            row, col = iota((128, 128), 0), iota((128, 128), 1)

            def system(i, j, rows, cols):
                view = cg[i : i + rows // 128, :, :, :, j * 128 : j * 128 + cols]
                return view.reshape(rows, cols).astype(f32)

            def exact_dot(a, b):
                return jnp.dot(a, b, precision=EXACT)

            def invert_diagonal():
                for j in range(4):
                    block = system(j, j, 128, 128)
                    parts[j] = jnp.where(row == col, 1.0 / jnp.where(row == col, block, 1.0), 0.0)

            def invert_level(level):
                same = (row >> (level + 1)) == (col >> (level + 1))
                upper_part = ((row >> level) + 1 == (col >> level)) & same
                steps = [exact_dot(jnp.where(upper_part, system(j, j, 128, 128), 0.0), parts[j]) for j in range(4)]
                for j in range(4):
                    parts[j] = parts[j] - exact_dot(parts[j], steps[j])

            def invert_halves():
                for j in range(2):
                    low, high = parts[2 * j], parts[2 * j + 1]
                    halves[j, 0:128, 0:128] = low
                    halves[j, 128:, 128:] = high
                    halves[j, 128:, 0:128] = jnp.zeros((128, 128), f32)
                    halves[j, 0:128, 128:] = -exact_dot(low, exact_dot(system(2 * j, 2 * j + 1, 128, 128), high))

            def keep_split(part, rows, cols):
                rounded = part.astype(bf16)
                inv[0, rows : rows + 256, cols : cols + 256] = rounded
                inv[1, rows : rows + 256, cols : cols + 256] = (part - rounded.astype(f32)).astype(bf16)

            def invert_whole():
                keep_split(halves[0], 0, 0)
                keep_split(halves[1], 256, 256)
                keep_split(-exact_dot(halves[0], exact_dot(system(0, 2, 256, 256), halves[1])), 0, 256)
                for n in range(2):
                    inv[n, 256:, 0:256] = jnp.zeros((256, 256), bf16)
                send(inv, inv, inverse_landed, partner)

            def consume(i):
                for half in range(2):
                    arrived(win.at[i // 4, i % 4, half], shared_landed + 2 * i + half)
                product(i)
                reduce_pairs(i)

            def start_u():
                arrived(ug.at[z, h, 0], picked_landed)
                u_gather.first()

            def start_c():
                arrived(cg.at[z, h, 0], corner_landed)
                pl.when(jnp.logical_not(is_owner))(lambda: arrived(cg.at[z, h, 1], corner_landed + 1))
                c_gather.first()

            def start_w():
                @pl.when(is_owner)
                def _():
                    wcb[0, 0, 1] = wcs[0:128, :]

                arrived(wcb.at[x, l, 0], part_landed)
                pl.when(jnp.logical_not(is_owner))(lambda: arrived(wcb.at[x, l, 1], part_landed + 1))
                w_gather.first()

            def third_u():
                u_gather.third()
                for n in range(3):
                    share_level(n)

            def finish_u():
                u_gather.finish()
                share_level(3)

            def finish_w():
                w_gather.finish()
                send(wcb.at[:, :, 0], wcb.at[:, :, 0], rows_landed, partner)

            send_corner()
            start_u()
            send_weights()
            start_c()
            transpose_features()
            u_gather.second()
            c_gather.second()
            start_w()
            w_gather.second()
            third_u()
            c_gather.third()
            consume(0)
            consume(1)
            w_gather.third()
            consume(2)
            consume(3)
            c_gather.finish()
            invert_diagonal()
            for n in range(3):
                invert_level(n)
            consume(4)
            for n in range(3, 6):
                invert_level(n)
            consume(5)
            invert_level(6)
            invert_halves()
            invert_whole()
            finish_u()
            consume(6)
            consume(7)
            finish_w()
            consume(8)
            consume(9)
            solve_rows(1)
            for i in range(10, STEPS):
                update_columns(i - 10)
                consume(i)
            send_pair()
            update_columns(6)
            update_columns(7)
            store_w.start()
            finish_hessian()

        for when, make in pending:
            if when is None:
                make().wait_send()
            else:
                pl.when(when)(lambda: make().wait_send())
        store_w.wait()
        store_h.wait()

    pl.when(k == 0)(lambda: run(0))
    pl.when(k == 1)(lambda: run(1))


def body(features, weights, u_rows, keep_pairs):
    bf16, f32 = jnp.bfloat16, jnp.float32
    anywhere = pl.BlockSpec(memory_space=pl.ANY)
    vmem = pl.BlockSpec(memory_space=pltpu.VMEM)
    return pl.pallas_call(
        kernel,
        out_shape=(
            jax.ShapeDtypeStruct((1024, LOCAL_COLS), bf16),
            jax.ShapeDtypeStruct((128, 1024), f32),
        ),
        in_specs=[anywhere, anywhere, anywhere, vmem],
        out_specs=(anywhere, anywhere),
        scratch_shapes=[
            pltpu.VMEM((2048, 1024), bf16),
            pltpu.VMEM((4, 1024, 512), bf16),
            pltpu.VMEM((4, 4, 2, 512, 128), bf16),
            pltpu.VMEM((4, 1024, 256), f32),
            pltpu.VMEM((3, 2, 1024, 128), bf16),
            pltpu.VMEM((1024, 128), bf16),
            pltpu.VMEM((2, 1024, 128), bf16),
            pltpu.VMEM((2, 1024, 128), bf16),
            pltpu.VMEM((2, 1024, 128), bf16),
            pltpu.VMEM((1024, 128), bf16),
            pltpu.VMEM((1024, LOCAL_COLS), bf16),
            pltpu.VMEM((64, LOCAL_COLS), f32),
            pltpu.VMEM((32, LOCAL_COLS), bf16),
            pltpu.VMEM((4, 2, 2, 32, LOCAL_COLS), bf16),
            pltpu.VMEM((4, 2, 2, 32, CORNER), bf16),
            pltpu.VMEM((1024, HALF), bf16),
            pltpu.VMEM((4, 2, 2, 128, HALF), bf16),
            pltpu.VMEM((1024, HALF), bf16),
            pltpu.VMEM((4, 128, 128), f32),
            pltpu.VMEM((2, 256, 256), f32),
            pltpu.VMEM((2, HALF, HALF), bf16),
            pltpu.VMEM((1, WIN), f32),
            pltpu.VMEM((4, 256, 128), bf16),
            pltpu.VMEM((2, 256, 1), jnp.int32),
            pltpu.VMEM((128, 1024), f32),
            pltpu.SemaphoreType.DMA((3,)),
            pltpu.SemaphoreType.DMA((2 * STEPS,)),
            pltpu.SemaphoreType.DMA((192,)),
            pltpu.SemaphoreType.DMA((112,)),
        ],
        compiler_params=pltpu.CompilerParams(
            collective_id=0, has_side_effects=True, vmem_limit_bytes=47 * 1024 * 1024
        ),
    )(features, weights, u_rows, keep_pairs.transpose(0, 2, 1))


def solution(mesh):
    in_specs = (P("dp", "mp"), P("mp", "dp"), P("mp", "dp"), P())
    out_specs = (P("mp", "dp"), P("dp", "mp"))
    return jax.shard_map(body, mesh=mesh, in_specs=in_specs, out_specs=out_specs, check_vma=False)
```

```python
import jax
import jax.numpy as jnp
from jax import lax
from jax.experimental import pallas as pl
from jax.experimental.pallas import tpu as pltpu
from jax.sharding import PartitionSpec as P

B = 512
PANELS = 2
WIN = 1024
TOKENS = 16384
HALF = WIN // 2
CORNER = HALF
LOCAL_COLS = 2048
STEPS = 16
LAG = 6
MESH = pl.DeviceIdType.MESH
EXACT = lax.Precision.HIGHEST


def iota(shape, dim):
    return lax.broadcasted_iota(jnp.int32, shape, dim)


def pruned_of(first, second):
    low = jnp.where(first != 0, 0, jnp.where(second != 1, 1, 2))
    high = jnp.where(second != 3, 3, jnp.where(first != 2, 2, 1))
    return low, high


def pruned_lanes(low, high):
    groups = low.shape[0]
    shape = (groups, 2 * groups)
    group, lane = iota(shape, 0), iota(shape, 1)
    own = jnp.where((lane & 1) == 0, low, high) + 4 * group
    return jnp.sum(jnp.where((lane >> 1) == group, own, 0), axis=0, keepdims=True)


def kept_lanes(low, high):
    groups = low.shape[0]
    shape = (groups, 4 * groups)
    group, lane = iota(shape, 0), iota(shape, 1)
    pruned = ((lane >> 2) == group) & (((lane & 3) == low) | ((lane & 3) == high))
    return 1.0 - jnp.sum(jnp.where(pruned, 1.0, 0.0), axis=0, keepdims=True)


def kernel(
    feat_hbm, w_hbm, u_hbm, pairs_ref, out_hbm, hess_hbm,
    feat, feat_t, win, acc, sums, to_pair, relay, from_left, from_right, from_pair,
    wv, uv, picked_rows, ug, cg, wcs, wcb, ev, parts, halves, inv, mask, picks, low_high, hout,
    local_sem, win_sem, send_sem, recv_sem,
):
    dp, mp = lax.axis_index("dp"), lax.axis_index("mp")
    x, l = lax.div(dp, 2), lax.rem(dp, 2)
    z, h, k = lax.div(mp, 4), lax.rem(lax.div(mp, 2), 2), lax.rem(mp, 2)
    is_source = mp == 0
    is_owner = dp == 0
    f32, bf16 = jnp.float32, jnp.bfloat16

    def at_mp(zz, hh, kk):
        return (dp, lax.rem(zz + 8, 4) * 4 + hh * 2 + kk)

    def at_dp(xx, ll):
        return (lax.rem(xx + 8, 4) * 2 + ll, mp)

    counter = [0]

    def take(n=1):
        counter[0] += n
        return counter[0] - n

    piece_landed = take(2 * STEPS)
    shared_landed = take(2 * STEPS)
    u_landed, c_landed, w_landed = take(5), take(5), take(5)
    picked_landed, corner_landed, part_landed = take(1), take(2), take(2)
    level_landed, inverse_landed, rows_landed = take(4), take(1), take(1)
    relay_landed, left_landed, right_landed, pair_landed = take(1), take(2), take(2), take(1)

    def remote(src, dst, sent, landed, device):
        return pltpu.make_async_remote_copy(
            src_ref=src, dst_ref=dst, send_sem=send_sem.at[sent], recv_sem=recv_sem.at[landed],
            device_id=device, device_id_type=MESH,
        )

    def arrived(dst, landed):
        remote(dst, dst, 0, landed, at_mp(z, h, 1 - k)).wait_recv()

    load_u = pltpu.make_async_copy(u_hbm, uv, local_sem.at[0])
    load_f = pltpu.make_async_copy(feat_hbm, feat, local_sem.at[1])
    load_w = pltpu.make_async_copy(w_hbm, wv, local_sem.at[2])
    load_u.start()

    def window_block(i, half):
        t, tq = divmod(i, 4)
        if t == 0 or t == 3:
            owner = lax.rem(x + (2 if t == 0 else 0), 4) * 2 + (l if half else 1 - l)
        else:
            owner = lax.rem(x + (3 if half else 1), 4) * 2 + (1 - l if t == 1 else l)
        column = pl.multiple_of(owner * 128, 128)
        return pltpu.make_async_copy(
            feat_hbm.at[pl.ds(tq * 512, 512), pl.ds(column, 128)], win.at[t, tq, half], win_sem.at[2 * i + half]
        )

    @pl.when(is_source)
    def _():
        for i in range(STEPS):
            for half in range(2):
                window_block(i, half).start()

    load_w.start()
    load_f.start()

    barrier = pltpu.get_barrier_semaphore()
    peers = [(lax.rem(dp + o, 8), mp) for o in range(1, 8)]
    peers += [(lax.rem(dp + o, 8), mp + 1 - 2 * k) for o in range(1, 8)]
    peers += [at_mp(z + 1, h, k), at_mp(z - 1, h, k), at_mp(z, 1 - h, k), at_mp(z, h, 1 - k)]
    for peer in peers:
        pl.semaphore_signal(barrier, inc=1, device_id=peer, device_id_type=MESH)

    wide = jnp.concatenate([pairs_ref[0], pairs_ref[1], pairs_ref[0], pairs_ref[1]], axis=0).astype(f32)
    tall = wide.T.astype(jnp.int32)
    for panel in range(PANELS):
        low, high = pruned_of(tall[:, 2 * panel : 2 * panel + 1], tall[:, 2 * panel + 1 : 2 * panel + 2])
        low_high[0, panel * 128 : (panel + 1) * 128, :] = low
        low_high[1, panel * 128 : (panel + 1) * 128, :] = high
    for c in range(4):
        low, high = low_high[0, c * 64 : (c + 1) * 64, :], low_high[1, c * 64 : (c + 1) * 64, :]
        picks[c] = (iota((256, 128), 0) == pruned_lanes(low, high)).astype(bf16)
        mask[:, c * 256 : (c + 1) * 256] = jnp.where(is_owner, kept_lanes(low, high), 1.0)

    own_groups = pl.ds(pl.multiple_of(mp * 16, 16), 16)
    own_rows = pruned_lanes(low_high[0, own_groups, :], low_high[1, own_groups, :])
    row_pick = (iota((64, 32), 0) == own_rows).astype(bf16)
    load_u.wait()
    picked = lax.dot_general(
        row_pick, uv[...].astype(bf16), (((0,), (0,)), ((), ())), preferred_element_type=f32
    ).astype(bf16)
    picked_rows[...] = picked

    @pl.when(k == 1)
    def _():
        ug[z, h, 1] = picked


    @pl.when(is_owner)
    def _():
        for c in range(4):
            cg[z, h, k, :, c * 128 : (c + 1) * 128] = jnp.dot(
                picked[:, c * 256 : (c + 1) * 256], picks[c], preferred_element_type=f32
            ).astype(bf16)

    pl.semaphore_wait(barrier, len(peers))

    def pick_weights():
        load_w.wait()

        @pl.when(is_owner)
        def _():
            for c in range(4):
                wcs[:, c * 128 : (c + 1) * 128] = jnp.dot(
                    wv[:, c * 256 : (c + 1) * 256], picks[c], preferred_element_type=f32
                ).astype(bf16)

    def transpose_features():
        load_f.wait()

        @pl.loop(0, 8)
        def _(tb):
            block = feat[pl.ds(pl.multiple_of(tb * 256, 256), 256), :]
            feat_t[lax.div(tb, 2), :, pl.ds(pl.multiple_of(lax.rem(tb, 2) * 256, 256), 256)] = block.T

    def product(i):
        t, tq = divmod(i, 4)

        @pl.loop(0, 2)
        def _(m):
            rows = pl.ds(pl.multiple_of(m * 512, 512), 512)
            columns = jnp.concatenate([win[t, tq, 0], win[t, tq, 1]], axis=1)
            part = jnp.dot(feat_t[tq, rows, :], columns, preferred_element_type=f32)
            if tq == 0:
                acc[t, rows, :] = part
            else:
                acc[t, rows, :] += part

    def add_to(slot, half, source):
        cols = pl.ds(half * 128, 128)

        @pl.loop(0, 4)
        def _(m):
            rows = pl.ds(pl.multiple_of(m * 256, 256), 256)
            acc[slot, rows, cols] += source[rows, :].astype(f32)

    def round_sum(slot, half):
        cols = pl.ds(half * 128, 128)

        @pl.loop(0, 4)
        def _(m):
            rows = pl.ds(pl.multiple_of(m * 256, 256), 256)
            sums[slot, half, rows, :] = acc[slot, rows, cols].astype(bf16)

    def update_columns(c):
        cols = pl.ds(c * 256, 256)
        factor = ug[:, :, :, :, cols].reshape(HALF, 256)
        updated = wv[:, cols].astype(f32) - jnp.dot(ev[...], factor, preferred_element_type=f32)
        if c < 4:
            updated = updated * mask[:, c * 256 : (c + 1) * 256]
        wv[:, cols] = updated.astype(bf16)

    def solve_rows(core):
        @pl.loop(0, 2)
        def _(m):
            lead = wcb[pl.ds(m * 2, 2), :, core].reshape(512, HALF)
            rows = pl.ds(pl.multiple_of(m * 512, 512), 512)
            first = lead[:, 0:256]
            ev[rows, 0:256] = (
                jnp.dot(first, inv[0, 0:256, 0:256], preferred_element_type=f32)
                + jnp.dot(first, inv[1, 0:256, 0:256], preferred_element_type=f32)
            ).astype(bf16)
            ev[rows, 256:] = (
                jnp.dot(lead, inv[0, :, 256:], preferred_element_type=f32)
                + jnp.dot(lead, inv[1, :, 256:], preferred_element_type=f32)
            ).astype(bf16)

    store_w = pltpu.make_async_copy(wv, out_hbm, local_sem.at[0])
    store_h = pltpu.make_async_copy(hout, hess_hbm, local_sem.at[1])

    def run(core):
        way = 1 - 2 * core
        pending = []
        sends = [0]
        partner = at_mp(z, h, 1 - core)
        right, left, onward = at_dp(x + 1, l), at_dp(x - 1, l), at_dp(x + way, l)

        def send(src, dst, landed, device, when=None):
            sent = sends[0]
            sends[0] += 1
            made = lambda ref: ref() if callable(ref) else ref
            make = lambda: remote(made(src), made(dst), sent, landed, device)
            if when is None:
                make().start()
            else:
                pl.when(when)(lambda: make().start())
            pending.append((when, make))

        def send_sum(slot, half):
            round_sum(slot, half)
            if half == 0:
                send(lambda: sums.at[slot, 0], lambda: from_left.at[slot - 1], left_landed + slot - 1, right)
            else:
                send(lambda: sums.at[slot, 1], lambda: from_right.at[slot - 1], right_landed + slot - 1, left)

        def reduce_pairs(i):
            if i == 3:
                round_sum(0, 0)
                round_sum(0, 1)
                send(lambda: sums.at[0], relay, relay_landed, onward)
            if i == 7:
                send_sum(1, 1 - core)
            if i == 9:
                arrived(relay, relay_landed)
                add_to(1, core, relay.at[0])
                send_sum(1, core)
            if i == 11:
                send_sum(2, 1 - core)
                add_to(2, core, relay.at[1])
                send_sum(2, core)

        def own_sum(n):
            arrived(from_left.at[n], left_landed + n)
            arrived(from_right.at[n], right_landed + n)
            total = acc[3, :, n * 128 : (n + 1) * 128] + from_left[n].astype(f32)
            return total + from_right[n].astype(f32)

        def send_pair():
            to_pair[...] = own_sum(0).astype(bf16)
            send(to_pair, from_pair, pair_landed, at_dp(x, 1 - l))

        def finish_hessian():
            total = own_sum(1)
            arrived(from_pair, pair_landed)
            hout[...] = ((total + from_pair[...].astype(f32)) * (2.0 / TOKENS)).T
            store_h.start()

        def send_corner():
            for o in range(7, -1, -1):
                device = (jnp.int32(o), mp + 1 - core)
                if o == 0:
                    if core == 0:
                        send(cg.at[z, h, 0], cg.at[z, h, 0], corner_landed, device, when=is_owner)
                else:
                    send(cg.at[z, h, core], cg.at[z, h, core], corner_landed + core, device, when=is_owner)

        def send_weights():
            pick_weights()
            for o in range(7, -1, -1):
                device = (jnp.int32(o), mp + 1 - core)
                part = wcs.at[pl.ds(o * 128, 128), :]
                target = wcb.at[o // 2, o % 2, core]
                if o == 0:
                    if core == 0:
                        send(part, target, part_landed, device, when=is_owner)
                else:
                    send(part, target, part_landed + core, device, when=is_owner)

        if core == 0:
            uneven = (z == 1) | (z == 3)
            follower = jnp.logical_not(is_source)
            early_set = jnp.where(z == 3, 1, 0)

            def piece(i, half):
                return win.at[i // 4, i % 4, half]

            def routes(half):
                step = 1 - 2 * half
                r = lax.rem(z * step + 4, 4)
                on_first = h == 0
                forward = (on_first & (r < 3)) | ((h == 1) & ((r == 1) | (r == 2)))
                cross = on_first & (r == 1)
                back = (h == 1) & (r == 1)
                return (
                    (forward, at_mp(z + step, h, 0), 0),
                    (cross, at_mp(z, 1, 0), 1),
                    (back, at_mp(z - step, h, 0), 2),
                )

            def copies(i, half):
                ref = piece(i, half)
                slot = 2 * i + half
                for when, device, kind in routes(half):
                    yield when, remote(ref, ref, 4 * slot + kind, piece_landed + slot, device)
                yield None, remote(ref, ref, 4 * slot + 3, shared_landed + slot, partner)

            def pass_on(i, half):
                for when, copy in copies(i, half):
                    if when is None:
                        copy.start()
                    else:
                        pl.when(when)(copy.start)

            sends[0] = 8 * STEPS

            def start_pieces(some):
                @pl.when(is_source)
                def _():
                    for i in some:
                        for half in range(2):
                            window_block(i, half).wait()
                            pass_on(i, half)

            send_corner()
            send(picked_rows, ug.at[z, h, 0], picked_landed, partner)
            start_pieces(range(4))
            send_weights()
            start_pieces(range(4, STEPS))
            transpose_features()

            def take_piece(i, half):
                arrived(piece(i, half), piece_landed + 2 * i + half)
                pass_on(i, half)

            def relay_all(trail, lag):
                for step in range(STEPS + lag):
                    if step < STEPS:
                        pl.when(follower)(lambda: take_piece(step, early_set))
                    if 0 <= step - trail < STEPS:
                        pl.when(follower)(lambda: take_piece(step - trail, 1 - early_set))
                    i = step - lag
                    if i >= 0:
                        product(i)
                        reduce_pairs(i)

            mark = (sends[0], len(pending))
            pl.when(uneven)(lambda: relay_all(LAG, LAG))
            sends[0] = mark[0]
            del pending[mark[1] :]
            pl.when(jnp.logical_not(uneven))(lambda: relay_all(0, 1))
            send_pair()
            arrived(inv, inverse_landed)
            arrived(wcb.at[:, :, 0], rows_landed)
            solve_rows(0)
            for n, zz in enumerate((z, z + 3, z + 1, z + 2)):
                arrived(ug.at[lax.rem(zz, 4)], level_landed + n)
            for c in range(8):
                update_columns(c)
            store_w.start()
            finish_hessian()
            for i in range(STEPS):
                for half in range(2):
                    for when, copy in copies(i, half):
                        if when is None:
                            copy.wait_send()
                        else:
                            pl.when(when)(copy.wait_send)
        else:

            class Gather:
                def __init__(self, buffer, landed, pos, line, device):
                    self.buffer, self.pos, self.line, self.device = buffer, pos, line, device
                    self.landed = landed
                    self.after = lax.rem(pos + 1, 4)
                    self.before = lax.rem(pos + 3, 4)
                    self.far = lax.rem(pos + 2, 4)

                def move(self, view, n, device):
                    send(view, view, self.landed + n, device)

                def first(self):
                    self.move(self.buffer.at[self.pos, self.line], 0, self.device(self.pos, 1 - self.line))

                def second(self):
                    arrived(self.buffer.at[self.pos, 1 - self.line], self.landed)
                    own = self.buffer.at[self.pos]
                    self.move(own, 1, self.device(self.pos + 1, self.line))
                    self.move(own, 2, self.device(self.pos - 1, self.line))

                def third(self):
                    arrived(self.buffer.at[self.before], self.landed + 1)
                    arrived(self.buffer.at[self.after], self.landed + 2)
                    self.move(self.buffer.at[self.before, 0], 3, self.device(self.pos + 1, self.line))
                    self.move(self.buffer.at[self.after, 1], 4, self.device(self.pos - 1, self.line))

                def finish(self):
                    arrived(self.buffer.at[self.far, 0], self.landed + 3)
                    arrived(self.buffer.at[self.far, 1], self.landed + 4)

            over_mp = lambda p, q: at_mp(p, q, 1)
            u_gather = Gather(ug, u_landed, z, h, over_mp)
            c_gather = Gather(cg, c_landed, z, h, over_mp)
            w_gather = Gather(wcb, w_landed, x, l, at_dp)
            levels = (u_gather.pos, u_gather.before, u_gather.after, u_gather.far)

            def share_level(n):
                send(ug.at[levels[n]], ug.at[levels[n]], level_landed + n, partner)

            row, col = iota((128, 128), 0), iota((128, 128), 1)

            def system(i, j, rows, cols):
                view = cg[i : i + rows // 128, :, :, :, j * 128 : j * 128 + cols]
                return view.reshape(rows, cols).astype(f32)

            def exact_dot(a, b):
                return jnp.dot(a, b, precision=EXACT)

            def invert_diagonal():
                for j in range(4):
                    block = system(j, j, 128, 128)
                    parts[j] = jnp.where(row == col, 1.0 / jnp.where(row == col, block, 1.0), 0.0)

            def invert_level(level):
                same = (row >> (level + 1)) == (col >> (level + 1))
                upper_part = ((row >> level) + 1 == (col >> level)) & same
                steps = [exact_dot(jnp.where(upper_part, system(j, j, 128, 128), 0.0), parts[j]) for j in range(4)]
                for j in range(4):
                    parts[j] = parts[j] - exact_dot(parts[j], steps[j])

            def invert_halves():
                for j in range(2):
                    low, high = parts[2 * j], parts[2 * j + 1]
                    halves[j, 0:128, 0:128] = low
                    halves[j, 128:, 128:] = high
                    halves[j, 128:, 0:128] = jnp.zeros((128, 128), f32)
                    halves[j, 0:128, 128:] = -exact_dot(low, exact_dot(system(2 * j, 2 * j + 1, 128, 128), high))

            def keep_split(part, rows, cols):
                rounded = part.astype(bf16)
                inv[0, rows : rows + 256, cols : cols + 256] = rounded
                inv[1, rows : rows + 256, cols : cols + 256] = (part - rounded.astype(f32)).astype(bf16)

            def invert_whole():
                keep_split(halves[0], 0, 0)
                keep_split(halves[1], 256, 256)
                keep_split(-exact_dot(halves[0], exact_dot(system(0, 2, 256, 256), halves[1])), 0, 256)
                for n in range(2):
                    inv[n, 256:, 0:256] = jnp.zeros((256, 256), bf16)
                send(inv, inv, inverse_landed, partner)

            def consume(i):
                for half in range(2):
                    arrived(win.at[i // 4, i % 4, half], shared_landed + 2 * i + half)
                product(i)
                reduce_pairs(i)

            def start_u():
                arrived(ug.at[z, h, 0], picked_landed)
                u_gather.first()

            def start_c():
                arrived(cg.at[z, h, 0], corner_landed)
                pl.when(jnp.logical_not(is_owner))(lambda: arrived(cg.at[z, h, 1], corner_landed + 1))
                c_gather.first()

            def start_w():
                @pl.when(is_owner)
                def _():
                    wcb[0, 0, 1] = wcs[0:128, :]

                arrived(wcb.at[x, l, 0], part_landed)
                pl.when(jnp.logical_not(is_owner))(lambda: arrived(wcb.at[x, l, 1], part_landed + 1))
                w_gather.first()

            def third_u():
                u_gather.third()
                for n in range(3):
                    share_level(n)

            def finish_u():
                u_gather.finish()
                share_level(3)

            def finish_w():
                w_gather.finish()
                send(wcb.at[:, :, 0], wcb.at[:, :, 0], rows_landed, partner)

            send_corner()
            start_u()
            send_weights()
            start_c()
            transpose_features()
            u_gather.second()
            c_gather.second()
            start_w()
            w_gather.second()
            third_u()
            c_gather.third()
            for i in range(4):
                consume(i)
            w_gather.third()
            consume(4)
            c_gather.finish()
            invert_diagonal()
            for n in range(3):
                invert_level(n)
            consume(5)
            for n in range(3, 6):
                invert_level(n)
            invert_level(6)
            invert_halves()
            invert_whole()
            finish_u()
            consume(6)
            consume(7)
            finish_w()
            consume(8)
            consume(9)
            solve_rows(1)
            for i in range(10, STEPS):
                update_columns(i - 10)
                consume(i)
            send_pair()
            update_columns(6)
            update_columns(7)
            store_w.start()
            finish_hessian()

        for when, make in pending:
            if when is None:
                make().wait_send()
            else:
                pl.when(when)(lambda: make().wait_send())
        store_w.wait()
        store_h.wait()

    pl.when(k == 0)(lambda: run(0))
    pl.when(k == 1)(lambda: run(1))


def body(features, weights, u_rows, keep_pairs):
    bf16, f32 = jnp.bfloat16, jnp.float32
    anywhere = pl.BlockSpec(memory_space=pl.ANY)
    vmem = pl.BlockSpec(memory_space=pltpu.VMEM)
    return pl.pallas_call(
        kernel,
        out_shape=(
            jax.ShapeDtypeStruct((1024, LOCAL_COLS), bf16),
            jax.ShapeDtypeStruct((128, 1024), f32),
        ),
        in_specs=[anywhere, anywhere, anywhere, vmem],
        out_specs=(anywhere, anywhere),
        scratch_shapes=[
            pltpu.VMEM((2048, 1024), bf16),
            pltpu.VMEM((4, 1024, 512), bf16),
            pltpu.VMEM((4, 4, 2, 512, 128), bf16),
            pltpu.VMEM((4, 1024, 256), f32),
            pltpu.VMEM((3, 2, 1024, 128), bf16),
            pltpu.VMEM((1024, 128), bf16),
            pltpu.VMEM((2, 1024, 128), bf16),
            pltpu.VMEM((2, 1024, 128), bf16),
            pltpu.VMEM((2, 1024, 128), bf16),
            pltpu.VMEM((1024, 128), bf16),
            pltpu.VMEM((1024, LOCAL_COLS), bf16),
            pltpu.VMEM((64, LOCAL_COLS), f32),
            pltpu.VMEM((32, LOCAL_COLS), bf16),
            pltpu.VMEM((4, 2, 2, 32, LOCAL_COLS), bf16),
            pltpu.VMEM((4, 2, 2, 32, CORNER), bf16),
            pltpu.VMEM((1024, HALF), bf16),
            pltpu.VMEM((4, 2, 2, 128, HALF), bf16),
            pltpu.VMEM((1024, HALF), bf16),
            pltpu.VMEM((4, 128, 128), f32),
            pltpu.VMEM((2, 256, 256), f32),
            pltpu.VMEM((2, HALF, HALF), bf16),
            pltpu.VMEM((1, WIN), f32),
            pltpu.VMEM((4, 256, 128), bf16),
            pltpu.VMEM((2, 256, 1), jnp.int32),
            pltpu.VMEM((128, 1024), f32),
            pltpu.SemaphoreType.DMA((3,)),
            pltpu.SemaphoreType.DMA((2 * STEPS,)),
            pltpu.SemaphoreType.DMA((192,)),
            pltpu.SemaphoreType.DMA((112,)),
        ],
        compiler_params=pltpu.CompilerParams(
            collective_id=0, has_side_effects=True, vmem_limit_bytes=47 * 1024 * 1024
        ),
    )(features, weights, u_rows, keep_pairs.transpose(0, 2, 1))


def solution(mesh):
    in_specs = (P("dp", "mp"), P("mp", "dp"), P("mp", "dp"), P())
    out_specs = (P("mp", "dp"), P("dp", "mp"))
    return jax.shard_map(body, mesh=mesh, in_specs=in_specs, out_specs=out_specs, check_vma=False)
```
